512 devices in a mesh: track: 64 (over y_hi, z, core), chan: 8 (over x, y_lo).
Axes of the slice: x: 4, y: 4 (y_hi: 2, y_lo: 2; y = y_hi * 2 + y_lo), z: 16, core: 2. Of those that a mesh axis runs over, the one named last changes fastest.
Arguments:
- radiance: bfloat16 [256, 30, 72, 128], P('track', None, 'chan'), may hold values from -600 to 600
- w_key: bfloat16 [72, 128, 128], P('chan'), may hold values from -0.5 to 0.5
- w_value: bfloat16 [72, 128, 128], P('chan'), may hold values from -0.5 to 0.5
- latent_query: bfloat16 [64, 512], replicated, may hold values from -6 to 6
- band_blocks: int32 [8, 48], replicated, may hold values from 0 to 71, as said below
- band_count: int32 [8], replicated, may hold values from 24 to 48
- valid_mask: int32 [256, 30, 9], P('track'), may hold values 0 or 1
- w_out: bfloat16 [512, 512], replicated, may hold values from -0.25 to 0.25
- conv_taps: float32 [3, 9, 512], replicated, may hold values from -2.5 to 2.5
- w_mix: bfloat16 [3, 512, 512], replicated, may hold values from -0.25 to 0.25
Outputs:
- cleared: bfloat16 [256, 30, 64, 512], P('track', None, 'chan')
The draws below stay inside these ranges and needn't reach their ends.
Inputs may be any that keep to these rules, and one draw needn't show every extreme that they name: `band_blocks`: within a row all entries are distinct; group g uses the first band_count[g] of them.
All inputs are finite; a program needn't handle non-finite values. No bound on the sum of `valid_mask` on one device may be relied on, other than what follows from the above.
Results may differ from the reference program's by a relative error of at most 0.0095.
Values may be sent and summed in bfloat16 or wider, within the bound.
A program may use at most 64 MiB of HBM per device.

```python
import math
import jax
import jax.numpy as jnp
from jax import lax

HEADS = 8
HEAD_DIM = 64
KV_HEADS = 2
D = 512
KVW = 128
GROUPS = 8
LAT_GROUP = 8
LAT = 64
CB = 128
NBLK = 72
MAXB = 48
SCAN = 30
CC_LAYERS = 3
LINES = 256


def band_lists(key):
    order_key, count_key, full_key, half_key = jax.random.split(jax.random.fold_in(key, 7), 4)
    row_keys = jax.random.split(order_key, GROUPS)
    blocks = jax.vmap(lambda row_key: jax.random.permutation(row_key, NBLK)[:MAXB])(row_keys)
    counts = jax.random.randint(count_key, (GROUPS,), MAXB // 2, MAXB + 1)
    full_group = jax.random.randint(full_key, (), 0, GROUPS)
    half_group = (full_group + 1 + jax.random.randint(half_key, (), 0, GROUPS - 1)) % GROUPS
    group_index = jnp.arange(GROUPS)
    counts = jnp.where(group_index == full_group, MAXB, jnp.where(group_index == half_group, MAXB // 2, counts))
    return (blocks.astype(jnp.int32), counts.astype(jnp.int32))


def draw_band_blocks(key, part):
    return band_lists(key)[0]


def draw_band_count(key, part):
    return band_lists(key)[1]


def draw_radiance(key, part):
    field_shape = (LINES, SCAN, NBLK, CB)
    noise_key, scale_key = jax.random.split(jax.random.fold_in(key, 11))
    block_scale = jnp.exp(jax.random.uniform(scale_key, (LINES, SCAN, NBLK, 1), jnp.float32, math.log(0.2), math.log(2.0)))
    noise_field = jax.random.normal(noise_key, field_shape, jnp.float32)
    return (noise_field * block_scale).astype(jnp.bfloat16)


def set_ends(values, own_key, low, largest):
    extent = values.shape
    index_at = [jax.random.randint(jax.random.fold_in(own_key, axis), (), 0, extent[axis]) for axis in range(len(extent))]
    values = values.at[tuple(index_at)].set(low)
    longest = extent.index(max(extent))
    index_at[longest] = (index_at[longest] + 1) % extent[longest]
    return values.at[tuple(index_at)].set(largest)


def block_levels(key, extent, pieces, least, largest):
    def one(axis_at, shards_of):
        draws = jax.random.uniform(jax.random.fold_in(jax.random.fold_in(key, 6), axis_at), (shards_of,), jnp.float32, least / len(pieces), largest / len(pieces))
        return jnp.repeat(jnp.exp(draws), extent[axis_at] // shards_of).reshape((-1,) + (1,) * (len(extent) - axis_at - 1))

    loudness = one(*pieces[0])
    for cut in pieces[1:]:
        loudness = loudness * one(*cut)
    return loudness


def normal_values(key, dims, spread, most, cuts=(), held_as=jnp.bfloat16):
    gain = block_levels(key, dims, cuts, -0.22, 0.18) if cuts else 1.0
    values = jax.random.normal(key, dims, jnp.float32) * spread * gain
    return jnp.minimum(jnp.maximum(values, -most), most).astype(held_as)


def setup_inputs(seed: int = 0) -> dict:
    splits = jax.random.split(jax.random.key(seed), 11)
    radiance = draw_radiance(jax.random.fold_in(splits[10], 71), 0)
    w_key = normal_values(splits[1], (NBLK, CB, KVW), CB ** -0.5, 0.5, ((0, 8),))
    w_value = normal_values(splits[2], (NBLK, CB, KVW), CB ** -0.5, 0.5, ((0, 8),))
    latent_query = normal_values(splits[3], (LAT, D), 1.0, 6.0)
    band_blocks = draw_band_blocks(jax.random.fold_in(splits[10], 71), 0)
    band_count = draw_band_count(jax.random.fold_in(splits[10], 71), 0)
    valid_mask = set_ends((jax.random.randint(splits[6], (LINES, SCAN, 9), 0, 4) < 3).astype(jnp.int32), jax.random.fold_in(splits[6], 1), 0, 1)
    w_out = normal_values(splits[7], (D, D), D ** -0.5, 0.25)
    conv_taps = normal_values(splits[8], (CC_LAYERS, 9, D), 0.35, 2.5, (), jnp.float32)
    w_mix = normal_values(splits[9], (CC_LAYERS, D, D), D ** -0.5, 0.25)
    return {"radiance": radiance, "w_key": w_key, "w_value": w_value, "latent_query": latent_query, "band_blocks": band_blocks, "band_count": band_count, "valid_mask": valid_mask, "w_out": w_out, "conv_taps": conv_taps, "w_mix": w_mix}


def band_table(band_blocks, band_count):
    slot_index = jnp.arange(band_blocks.shape[1], dtype=jnp.int32)
    in_use = slot_index[None, :] < band_count[:, None]
    block_index = jnp.arange(NBLK, dtype=jnp.int32)
    matches = (band_blocks[:, :, None] == block_index[None, None, :]) & in_use[:, :, None]
    return jnp.any(matches, axis=1)

def project_blocks(radiance_rows, w_key, w_value):
    values32 = radiance_rows.astype(jnp.float32)
    key_rows = jnp.einsum('fnc,nck->fnk', values32, w_key.astype(jnp.float32), precision=lax.Precision.HIGHEST).astype(jnp.bfloat16)
    inverse = lax.rsqrt(lax.optimization_barrier(jnp.mean(values32 * values32, axis=-1, keepdims=True)) + 1e-05)
    normed = (values32 * inverse).astype(jnp.bfloat16)
    value_rows = jnp.einsum('fnc,nck->fnk', normed.astype(jnp.float32), w_value.astype(jnp.float32), precision=lax.Precision.HIGHEST).astype(jnp.bfloat16)
    return (key_rows, value_rows)

def attend(queries, key_rows, value_rows, allowed_lat):
    repeat = HEADS // KV_HEADS
    footprints, block_count = (key_rows.shape[0], key_rows.shape[1])
    query_heads = queries.astype(jnp.float32).reshape(queries.shape[0], KV_HEADS, repeat, HEAD_DIM)
    key_heads = key_rows.astype(jnp.float32).reshape(footprints, block_count, KV_HEADS, HEAD_DIM)
    value_heads = value_rows.astype(jnp.float32).reshape(footprints, block_count, KV_HEADS, HEAD_DIM)
    scores = jnp.einsum('lgrd,fngd->flgrn', query_heads, key_heads, precision=lax.Precision.HIGHEST) * HEAD_DIM ** (-0.5)
    allowed_now = allowed_lat[None, :, None, None, :]
    scores = jnp.where(allowed_now, scores, -1e+30)
    peak = lax.optimization_barrier(jnp.max(scores, axis=-1, keepdims=True))
    weights = jnp.where(allowed_now, jnp.exp(scores - peak), 0.0)
    weight_sum = lax.optimization_barrier(jnp.sum(weights, axis=-1, keepdims=True))
    weighted = jnp.einsum('flgrn,fngd->flgrd', weights, value_heads, precision=lax.Precision.HIGHEST) / weight_sum
    return weighted.reshape(footprints, queries.shape[0], HEADS * HEAD_DIM).astype(jnp.bfloat16)

def add_output(queries, attended, w_out):
    mixed_term = jnp.dot(attended.reshape(-1, attended.shape[-1]), w_out, preferred_element_type=jnp.float32)
    mixed_term = mixed_term.reshape(attended.shape)
    return (queries.astype(jnp.float32)[None] + mixed_term).astype(jnp.bfloat16)

def clear_layer(latents, valid_mask, taps, w_mix):
    line_count, scan_width = (latents.shape[0], latents.shape[1])
    padded = jnp.pad(latents, ((1, 1), (1, 1), (0, 0), (0, 0)))

    def one_line(line_index):
        window = lax.dynamic_slice_in_dim(padded, line_index, 3, 0)
        validity = lax.dynamic_index_in_dim(valid_mask, line_index, 0, keepdims=False).astype(jnp.float32)
        gathered = jnp.zeros(latents.shape[1:], jnp.float32)
        for offset in range(9):
            row_step, col_step = (offset // 3, offset % 3)
            beside = window[row_step, col_step:col_step + scan_width].astype(jnp.float32)
            gathered = gathered + validity[:, offset][:, None, None] * taps[offset][None, None, :] * beside
        mixed_term = gathered.astype(jnp.bfloat16)
        update = jnp.dot(mixed_term.reshape(-1, mixed_term.shape[-1]), w_mix, preferred_element_type=jnp.float32).reshape(gathered.shape)
        centre = window[1, 1:1 + scan_width].astype(jnp.float32)
        return (centre + update).astype(jnp.bfloat16)
    return lax.map(one_line, jnp.arange(line_count, dtype=jnp.int32))

def reference(radiance, w_key, w_value, latent_query, band_blocks, band_count, valid_mask, w_out, conv_taps, w_mix):
    allowed_lat = jnp.repeat(band_table(band_blocks, band_count), LAT_GROUP, axis=0)

    def one_line(line_rows):
        key_rows, value_rows = project_blocks(line_rows, w_key, w_value)
        attended = attend(latent_query, key_rows, value_rows, allowed_lat)
        return add_output(latent_query, attended, w_out)
    latents = lax.map(one_line, radiance)
    for layer_index in range(CC_LAYERS):
        latents = clear_layer(latents, valid_mask, conv_taps[layer_index], w_mix[layer_index])
    return latents
```

```python
import functools

import jax
import jax.numpy as jnp
from jax import lax
from jax.experimental import pallas as pl
from jax.experimental.pallas import tpu as pltpu
from jax.sharding import PartitionSpec as P

HEADS = 8
HEAD_DIM = 64
NBLK = 72
LAYERS = 3
NX, NY = 4, 2
CHAN = NX * NY
LINES, SCAN = 4, 30
PER = LINES * SCAN // CHAN
ROWS = 16
BLK = NBLK // CHAN
LAT, D, CB = 64, 512, 128
LG = LAT // CHAN
CHUNKS = 3
PC = PER // CHUNKS
MASKED = -1e30
MESH = pl.DeviceIdType.MESH
OFFSETS = ((2, 1), (2, 0), (1, 1), (3, 1), (1, 0), (3, 0), (0, 1))


def nt_dot(a, b):
    return lax.dot_general(a, b, (((1,), (1,)), ((), ())), preferred_element_type=jnp.float32)


def kernel(
    tracks, rad, wk, wv, q, bb, cnt, vm, w_out, taps, w_mix, out,
    xf, kv_send, kv_recv, kf, vf, qbt, bias, att, lsend, lrecv, grid_f, tb, st, hsend, hrecv,
    kv_ssem, kv_rsem, l_ssem, l_rsem, h_ssem, h_rsem, own_sem,
):
    track, me = lax.axis_index("track"), lax.axis_index("chan")
    x, y = me // NY, me % NY
    up, down = (track + tracks - 1) % tracks, (track + 1) % tracks

    def to_peer(o):
        return ((x + o[0]) % NX) * NY + (y + o[1]) % NY

    def from_peer(o):
        return ((x + NX - o[0]) % NX) * NY + (y + NY - o[1]) % NY

    barrier = pltpu.get_barrier_semaphore()
    for o in OFFSETS:
        pl.semaphore_signal(barrier, inc=1, device_id=(track, to_peer(o)), device_id_type=MESH)
    for other in (up, down):
        pl.semaphore_signal(barrier, inc=1, device_id=(other, me), device_id_type=MESH)

    xf[pl.ds(SCAN * BLK * LINES, 72), :] = jnp.zeros((72, CB), jnp.float32)
    xf[pl.ds(0, SCAN * BLK * LINES), :] = (
        rad[...].astype(jnp.float32).reshape(SCAN * BLK * LINES, CB)
    )

    for b in range(BLK):
        rows = jnp.concatenate(
            [
                xf[pl.ds((j % 2) * BLK * LINES + b * LINES + j // 2, ROWS, stride=2 * BLK * LINES), :]
                for j in range(CHAN)
            ],
            axis=0,
        )
        inverse = lax.rsqrt(jnp.mean(rows * rows, axis=-1, keepdims=True) + 1e-05)
        normed = (rows * inverse).astype(jnp.bfloat16)
        keys = jnp.dot(rows.astype(jnp.bfloat16), wk[b], preferred_element_type=jnp.float32)
        values = jnp.dot(normed, wv[b], preferred_element_type=jnp.float32)
        kv_send[:, 0, b] = keys.astype(jnp.bfloat16).reshape(CHAN, ROWS, CB)
        kv_send[:, 1, b] = values.astype(jnp.bfloat16).reshape(CHAN, ROWS, CB)

    pl.semaphore_wait(barrier, len(OFFSETS) + 2)

    def kv_copy(o, i):
        return pltpu.make_async_remote_copy(
            src_ref=kv_send.at[to_peer(o)],
            dst_ref=kv_recv.at[me],
            send_sem=kv_ssem.at[i],
            recv_sem=kv_rsem.at[i],
            device_id=(track, to_peer(o)),
            device_id_type=MESH,
        )

    for i, o in enumerate(OFFSETS):
        kv_copy(o, i).start()

    lane = lax.broadcasted_iota(jnp.int32, (LAT, CB), 1)
    low = lane < HEAD_DIM
    for h in range(HEADS):
        e = h // 4
        part = q[:, (h // 2) * CB : (h // 2 + 1) * CB].astype(jnp.float32) * HEAD_DIM**-0.5
        if h % 2 != e:
            part = pltpu.roll(part, HEAD_DIM, 1)
        part = jnp.where(low if e == 0 else jnp.logical_not(low), part, 0.0)
        qbt[h * LAT : (h + 1) * LAT, :] = part.astype(jnp.bfloat16)

    group = lax.broadcasted_iota(jnp.int32, (CHAN, 48), 0)
    slot = lax.broadcasted_iota(jnp.int32, (CHAN, 48), 1)
    used = jnp.zeros((CHAN, 48), jnp.int32)
    for g in range(CHAN):
        used = jnp.where(group == g, cnt[g], used)
    blocks = jnp.where(slot < used, bb[...], -1)
    block_of = lax.broadcasted_iota(jnp.int32, (CHAN, CB), 1)
    allowed = jnp.full((CHAN, CB), MASKED, jnp.float32)
    for j in range(48):
        allowed = jnp.where(blocks[:, j : j + 1] == block_of, 0.0, allowed)
    for g in range(CHAN):
        bias[g * LG : (g + 1) * LG, :] = jnp.broadcast_to(allowed[g : g + 1], (LG, CB))

    for c in range(LAYERS):
        for k in range(9):
            tb[c * 9 + k] = jnp.broadcast_to(taps[k, c : c + 1], (LG, D))
    for s in range(2):
        for edge in (0, SCAN + 1):
            grid_f[s, :, edge] = jnp.zeros((LINES + 2, LG, D), jnp.float32)
    kf[pl.ds(NBLK * ROWS, (CB - NBLK) * ROWS), :] = jnp.zeros(((CB - NBLK) * ROWS, CB), jnp.float32)
    vf[pl.ds(NBLK * ROWS, (CB - NBLK) * ROWS), :] = jnp.zeros(((CB - NBLK) * ROWS, CB), jnp.float32)

    def spread(ref, s):
        at = pl.ds(pl.multiple_of(s * (BLK * ROWS), BLK * ROWS), BLK * ROWS)
        kf[at, :] = ref[s, 0].astype(jnp.float32).reshape(BLK * ROWS, CB)
        vf[at, :] = ref[s, 1].astype(jnp.float32).reshape(BLK * ROWS, CB)

    spread(kv_send, me)
    for i in reversed(range(len(OFFSETS))):
        o = OFFSETS[i]
        kv_copy(o, i).wait_recv()
        spread(kv_recv, from_peer(o))

    line_me, side_me = me // 2, me % 2

    def lat_copy(o, i, c):
        return pltpu.make_async_remote_copy(
            src_ref=lsend.at[to_peer(o), pl.ds(c * PC, PC)],
            dst_ref=lrecv.at[line_me, pl.ds(c * PC, PC), side_me],
            send_sem=l_ssem.at[c, i],
            recv_sem=l_rsem.at[c, i],
            device_id=(track, to_peer(o)),
            device_id_type=MESH,
        )

    def own_copy(c):
        return pltpu.make_async_copy(
            lsend.at[me, pl.ds(c * PC, PC)],
            lrecv.at[line_me, pl.ds(c * PC, PC), side_me],
            own_sem.at[c],
        )

    ones = jnp.ones((CB, CB), jnp.bfloat16)
    low_v = lax.broadcasted_iota(jnp.int32, (CB, CB), 1) < HEAD_DIM
    for c in range(CHUNKS):

        def attend(mm, _):
            m = c * PC + mm
            keys = kf[pl.ds(m, CB, stride=ROWS), :].astype(jnp.bfloat16)
            values = vf[pl.ds(m, CB, stride=ROWS), :]
            swapped = pltpu.roll(values, HEAD_DIM, 1)
            scores = nt_dot(qbt[...], keys).reshape(HEADS, LAT, CB) + bias[...][None]
            peak = jnp.max(scores, axis=-1, keepdims=True)
            weights = jnp.exp(scores - peak).astype(jnp.bfloat16)
            for e in range(2):
                pair = jnp.where(low_v, values, swapped) if e == 0 else jnp.where(low_v, swapped, values)
                both = jnp.concatenate([pair.astype(jnp.bfloat16), ones], axis=1)
                sums = jnp.dot(
                    weights[e * 4 : (e + 1) * 4].reshape(4 * LAT, CB), both,
                    preferred_element_type=jnp.float32,
                )
                for t in range(2):
                    a, b = sums[2 * t * LAT : (2 * t + 1) * LAT], sums[(2 * t + 1) * LAT : (2 * t + 2) * LAT]
                    top = jnp.where(low, a[:, :CB], b[:, :CB])
                    bottom = jnp.where(low, a[:, CB:], b[:, CB:])
                    at = (e * 2 + t) * CB
                    att[mm, :, at : at + CB] = (top / bottom).astype(jnp.bfloat16)
            return 0

        lax.fori_loop(0, PC, attend, 0)
        mixed = jnp.dot(
            att[...].reshape(PC * LAT, D), w_out[...], preferred_element_type=jnp.float32
        ).reshape(PC, LAT, D)
        latents = (q[...].astype(jnp.float32)[None] + mixed).reshape(PC, CHAN, LG, D)
        for g in range(CHAN):
            lsend[g, c * PC : (c + 1) * PC] = latents[:, g].astype(jnp.bfloat16)
        for i, o in enumerate(OFFSETS):
            lat_copy(o, i, c).start()
        own_copy(c).start()

    for c in range(CHUNKS):
        own_copy(c).wait()
        for i, o in enumerate(OFFSETS):
            src = from_peer(o)
            pltpu.make_async_remote_copy(
                src_ref=lsend.at[0, pl.ds(c * PC, PC)],
                dst_ref=lrecv.at[src // 2, pl.ds(c * PC, PC), src % 2],
                send_sem=l_ssem.at[c, i],
                recv_sem=l_rsem.at[c, i],
                device_id=(track, to_peer(o)),
                device_id_type=MESH,
            ).wait_recv()

    def halo_copy(c, way):
        return pltpu.make_async_remote_copy(
            src_ref=hsend.at[c, way],
            dst_ref=hrecv.at[c, way],
            send_sem=h_ssem.at[c, way],
            recv_sem=h_rsem.at[c, way],
            device_id=((up, down)[way], me),
            device_id_type=MESH,
        )

    for way, l in ((0, 0), (1, LINES - 1)):
        hsend[0, way] = lrecv[l].reshape(SCAN, LG, D)
        halo_copy(0, way).start()
    for l in range(LINES):
        grid_f[0, l + 1, 1 : SCAN + 1] = lrecv[l].reshape(SCAN, LG, D).astype(jnp.float32)

    for c in range(LAYERS):
        now, later = c % 2, (c + 1) % 2

        def clear_line(l):
            def column(i, _):
                for dp in range(2):
                    p = 2 * i + dp
                    scale = [vm[k, l, p].astype(jnp.float32) for k in range(9)]
                    for f in range(D // CB):
                        lanes = slice(f * CB, (f + 1) * CB)
                        total = None
                        for k in range(9):
                            term = (scale[k] * tb[c * 9 + k, :, lanes]) * grid_f[
                                now, l + k // 3, p + k % 3, :, lanes
                            ]
                            total = term if total is None else total + term
                        st[p, :, lanes] = total.astype(jnp.bfloat16)
                return 0

            lax.fori_loop(0, SCAN // 2, column, 0)
            update = jnp.dot(
                st[...].reshape(SCAN * LG, D), w_mix[c], preferred_element_type=jnp.float32
            ).reshape(SCAN, LG, D)
            return (grid_f[now, l + 1, 1 : SCAN + 1] + update).astype(jnp.bfloat16)

        def keep(l, cleared):
            if c == LAYERS - 1:
                out[l] = cleared
            else:
                grid_f[later, l + 1, 1 : SCAN + 1] = cleared.astype(jnp.float32)

        for l in range(1, LINES - 1):
            keep(l, clear_line(l))
        for way, edge, outside in ((1, 0, 0), (0, LINES + 1, tracks - 1)):
            halo_copy(c, way).wait_recv()
            beside = hrecv[c, way].astype(jnp.float32)
            grid_f[now, edge, 1 : SCAN + 1] = jnp.where(track == outside, 0.0, beside)
        for way, l in ((0, 0), (1, LINES - 1)):
            cleared = clear_line(l)
            keep(l, cleared)
            if c < LAYERS - 1:
                hsend[c + 1, way] = cleared
                halo_copy(c + 1, way).start()

    for i, o in enumerate(OFFSETS):
        kv_copy(o, i).wait_send()
        for c in range(CHUNKS):
            lat_copy(o, i, c).wait_send()
    for c in range(LAYERS):
        for way in range(2):
            halo_copy(c, way).wait_send()


def local(tracks, radiance, w_key, w_value, latent_query, band_blocks, band_count, valid_mask, w_out, conv_taps, w_mix):
    vmem = pl.BlockSpec(memory_space=pltpu.VMEM)
    smem = pl.BlockSpec(memory_space=pltpu.SMEM)
    bf16, f32 = jnp.bfloat16, jnp.float32
    dma = pltpu.SemaphoreType.DMA
    peers = len(OFFSETS)
    return pl.pallas_call(
        functools.partial(kernel, tracks),
        out_shape=jax.ShapeDtypeStruct((LINES, SCAN, LG, D), bf16),
        in_specs=[vmem, vmem, vmem, vmem, vmem, smem, smem, vmem, vmem, vmem],
        out_specs=vmem,
        scratch_shapes=[
            pltpu.VMEM((SCAN * BLK * LINES + 72, CB), f32),
            pltpu.VMEM((CHAN, 2, BLK, ROWS, CB), bf16),
            pltpu.VMEM((CHAN, 2, BLK, ROWS, CB), bf16),
            pltpu.VMEM((CB * ROWS, CB), f32),
            pltpu.VMEM((CB * ROWS, CB), f32),
            pltpu.VMEM((HEADS * LAT, CB), bf16),
            pltpu.VMEM((LAT, CB), f32),
            pltpu.VMEM((PC, LAT, D), bf16),
            pltpu.VMEM((CHAN, PER, LG, D), bf16),
            pltpu.VMEM((LINES, PER, 2, LG, D), bf16),
            pltpu.VMEM((2, LINES + 2, SCAN + 2, LG, D), f32),
            pltpu.VMEM((LAYERS * 9, LG, D), f32),
            pltpu.VMEM((SCAN, LG, D), bf16),
            pltpu.VMEM((LAYERS, 2, SCAN, LG, D), bf16),
            pltpu.VMEM((LAYERS, 2, SCAN, LG, D), bf16),
            dma((peers,)), dma((peers,)),
            dma((CHUNKS, peers)), dma((CHUNKS, peers)),
            dma((LAYERS, 2)), dma((LAYERS, 2)),
            dma((CHUNKS,)),
        ],
        compiler_params=pltpu.CompilerParams(
            collective_id=0, has_side_effects=True, vmem_limit_bytes=60 * 1024 * 1024
        ),
    )(
        jnp.transpose(radiance, (1, 2, 0, 3)), w_key, w_value, latent_query, band_blocks, band_count,
        jnp.transpose(valid_mask, (2, 0, 1)), w_out, jnp.transpose(conv_taps, (1, 0, 2)), w_mix,
    )


def solution(mesh):
    return jax.shard_map(
        functools.partial(local, mesh.shape["track"]),
        mesh=mesh,
        in_specs=(
            P("track", None, "chan", None),
            P("chan", None, None),
            P("chan", None, None),
            P(),
            P(),
            P(),
            P("track", None, None),
            P(),
            P(),
            P(),
        ),
        out_specs=P("track", None, "chan", None),
        check_vma=False,
    )
```

```python
import functools

import jax
import jax.numpy as jnp
from jax import lax
from jax.experimental import pallas as pl
from jax.experimental.pallas import tpu as pltpu
from jax.sharding import PartitionSpec as P

HEADS = 8
HEAD_DIM = 64
NBLK = 72
LAYERS = 3
NX, NY = 4, 2
CHAN = NX * NY
LINES, SCAN = 4, 30
WIDE = 32
PER = LINES * SCAN // CHAN
ROWS = 16
BLK = NBLK // CHAN
LAT, D, CB = 64, 512, 128
FT = D // CB
LG = LAT // CHAN
MAXB = 48
HALF = LG // 2
STEP = 4
CHUNKS = ROWS // STEP
MASKED = -1e30
MESH = pl.DeviceIdType.MESH
OFFSETS = ((2, 1), (2, 0), (1, 1), (3, 1), (1, 0), (3, 0), (0, 1))
BF16, F32 = jnp.bfloat16, jnp.float32


def nt_dot(a, b):
    return lax.dot_general(a, b, (((1,), (1,)), ((), ())), preferred_element_type=F32)


def chunk_at(c):
    return pl.ds(c * STEP, min(STEP, PER - c * STEP))


def kernel(
    tracks, rad_h, wk_h, wv_h, q_h, bb_h, cnt_h, vm_h, w_out_h, taps_h, w_mix_h, out_h,
    rad, wk, wv, q, bb, cnt, vm, w_out, taps, w_mix,
    xf, kv_send, kv_recv, kf, vf, qbt, bias, att, lsend, lrecv, near,
    vmf, mb, coef, turn, grid_f, st, hsend, hrecv, last, outb,
    in_sem, kv_ssem, kv_rsem, l_ssem, l_rsem, n_ssem, n_rsem, h_ssem, h_rsem, out_sem,
):
    track, me = lax.axis_index("track"), lax.axis_index("chan")
    x, y = me // NY, me % NY
    up, down = (track + tracks - 1) % tracks, (track + 1) % tracks
    ways = (up, down)

    def to_peer(o):
        return ((x + o[0]) % NX) * NY + (y + o[1]) % NY

    def from_peer(o):
        return ((x + NX - o[0]) % NX) * NY + (y + NY - o[1]) % NY

    barrier = pltpu.get_barrier_semaphore()
    for o in OFFSETS:
        pl.semaphore_signal(barrier, inc=1, device_id=(track, to_peer(o)), device_id_type=MESH)
    for other in ways:
        pl.semaphore_signal(barrier, inc=1, device_id=(other, me), device_id_type=MESH)

    loads = [
        pltpu.make_async_copy(src, dst, in_sem.at[i])
        for i, (src, dst) in enumerate(
            (
                (rad_h, rad), (wk_h, wk), (wv_h, wv), (q_h, q), (bb_h, bb), (cnt_h, cnt),
                (vm_h, vm), (taps_h, taps), (w_out_h, w_out), (w_mix_h, w_mix),
            )
        )
    ]
    for load in loads:
        load.start()

    xf[pl.ds(SCAN * BLK * LINES, 72), :] = jnp.zeros((72, CB), F32)
    loads[0].wait()
    xf[pl.ds(0, SCAN * BLK * LINES), :] = rad[...].astype(F32).reshape(SCAN * BLK * LINES, CB)
    loads[1].wait()
    loads[2].wait()

    for b in range(BLK):
        rows = jnp.concatenate(
            [
                xf[pl.ds((j % 2) * BLK * LINES + b * LINES + j // 2, ROWS, stride=2 * BLK * LINES), :]
                for j in range(CHAN)
            ],
            axis=0,
        )
        inverse = lax.rsqrt(jnp.mean(rows * rows, axis=-1, keepdims=True) + 1e-05)
        normed = (rows * inverse).astype(BF16)
        keys = jnp.dot(rows.astype(BF16), wk[b], preferred_element_type=F32)
        values = jnp.dot(normed, wv[b], preferred_element_type=F32)
        kv_send[:, :, 0, b] = keys.astype(BF16).reshape(CHAN, 2, 8, CB)
        kv_send[:, :, 1, b] = values.astype(BF16).reshape(CHAN, 2, 8, CB)

    pl.semaphore_wait(barrier, len(OFFSETS) + 2)

    def kv_copy(o, i, c):
        return pltpu.make_async_remote_copy(
            src_ref=kv_send.at[to_peer(o), c],
            dst_ref=kv_recv.at[me, c],
            send_sem=kv_ssem.at[c, i],
            recv_sem=kv_rsem.at[c, i],
            device_id=(track, to_peer(o)),
            device_id_type=MESH,
        )

    for c in range(2):
        for i, o in enumerate(OFFSETS):
            kv_copy(o, i, c).start()

    for load in loads[3:]:
        load.wait()
    lane = lax.broadcasted_iota(jnp.int32, (LAT, CB), 1)
    low = lane < HEAD_DIM
    for h in range(HEADS):
        e = h // 4
        part = q[:, (h // 2) * CB : (h // 2 + 1) * CB].astype(F32) * HEAD_DIM**-0.5
        if h % 2 != e:
            part = pltpu.roll(part, HEAD_DIM, 1)
        part = jnp.where(low if e == 0 else jnp.logical_not(low), part, 0.0)
        qbt[h * LAT : (h + 1) * LAT, :] = part.astype(BF16)

    group = lax.broadcasted_iota(jnp.int32, (CHAN, MAXB), 0)
    slot = lax.broadcasted_iota(jnp.int32, (CHAN, MAXB), 1)
    used = jnp.zeros((CHAN, MAXB), jnp.int32)
    for g in range(CHAN):
        used = jnp.where(group == g, cnt[g], used)
    blocks = jnp.where(slot < used, bb[...], -1)
    block_of = lax.broadcasted_iota(jnp.int32, (CHAN, CB), 1)
    allowed = jnp.full((CHAN, CB), MASKED, F32)
    for j in range(MAXB):
        allowed = jnp.where(blocks[:, j : j + 1] == block_of, 0.0, allowed)
    for g in range(CHAN):
        bias[g * LG : (g + 1) * LG, :] = jnp.broadcast_to(allowed[g : g + 1], (LG, CB))

    kf[:, pl.ds(NBLK * 8, (CB - NBLK) * 8), :] = jnp.zeros((2, (CB - NBLK) * 8, CB), F32)
    vf[:, pl.ds(NBLK * 8, (CB - NBLK) * 8), :] = jnp.zeros((2, (CB - NBLK) * 8, CB), F32)

    def spread(ref, s, c):
        at = pl.ds(pl.multiple_of(s * (BLK * 8), BLK * 8), BLK * 8)
        kf[c, at, :] = ref[s, c, 0].astype(F32).reshape(BLK * 8, CB)
        vf[c, at, :] = ref[s, c, 1].astype(F32).reshape(BLK * 8, CB)

    for c in range(2):
        spread(kv_send, me, c)

    vmf[...] = jnp.zeros((CB, CB), F32)
    for k in range(9):
        vmf[k * LINES : (k + 1) * LINES, 0:SCAN] = vm[k].astype(F32)
    turned = vmf[...].T
    for l in range(LINES):
        for k in range(9):
            col = turned[:WIDE, k * LINES + l : k * LINES + l + 1]
            mb[l, k] = jnp.broadcast_to(col, (WIDE, CB))

    def coefficients(l, _):
        for c in range(LAYERS):
            for f in range(FT):
                for k in range(9):
                    coef[c, l, f, k] = mb[l, k] * taps[k, c : c + 1, f * CB : (f + 1) * CB]
        return 0

    lax.fori_loop(0, LINES, coefficients, 0)

    def borders(l, _):
        for s in range(2):
            for i in range(LG):
                grid_f[s, l, i, :, 0:8] = jnp.zeros((FT, 8, CB), F32)
                grid_f[s, l, i, :, 8 + WIDE : 16 + WIDE] = jnp.zeros((FT, 8, CB), F32)
        turn[l, :, SCAN * LG : WIDE * LG] = jnp.zeros((FT, (WIDE - SCAN) * LG, CB), F32)
        return 0

    lax.fori_loop(0, LINES + 2, borders, 0)

    line_me, side_me = me // 2, me % 2

    def lat_copy(o, i, c):
        return pltpu.make_async_remote_copy(
            src_ref=lsend.at[to_peer(o), chunk_at(c)],
            dst_ref=lrecv.at[line_me, chunk_at(c), side_me],
            send_sem=l_ssem.at[c, i],
            recv_sem=l_rsem.at[c, me],
            device_id=(track, to_peer(o)),
            device_id_type=MESH,
        )

    def own_copy(c):
        return pltpu.make_async_copy(
            lsend.at[me, chunk_at(c)],
            lrecv.at[line_me, chunk_at(c), side_me],
            l_rsem.at[c, me],
        )

    def await_latents(s, c):
        pltpu.make_async_copy(
            lsend.at[s, chunk_at(c)], lrecv.at[s // 2, chunk_at(c), s % 2], l_rsem.at[c, s]
        ).wait()

    def near_copy(c, way):
        return pltpu.make_async_remote_copy(
            src_ref=lrecv.at[way * (LINES - 1), chunk_at(c)],
            dst_ref=near.at[way, chunk_at(c)],
            send_sem=n_ssem.at[c, way],
            recv_sem=n_rsem.at[c, way],
            device_id=(ways[way], me),
            device_id_type=MESH,
        )

    def forward(c):
        for way in range(2):
            for s in range(2):
                await_latents(way * (CHAN - 2) + s, c)
            near_copy(c, way).start()

    ones = jnp.ones((CB, CB), BF16)
    low_v = lax.broadcasted_iota(jnp.int32, (CB, CB), 1) < HEAD_DIM

    def attend(c, n):
        def some(pair, _):
            tags = [(mm, e) for mm in range(n) for e in range(2)]
            at = [c % 2 * STEP + pair * n + mm for mm in range(n)]
            keys = [kf[c // 2, pl.ds(a, CB, stride=8), :].astype(BF16) for a in at]
            values = [vf[c // 2, pl.ds(a, CB, stride=8), :] for a in at]
            swapped = [pltpu.roll(v, HEAD_DIM, 1) for v in values]
            both = {
                (mm, e): jnp.concatenate(
                    [
                        (
                            jnp.where(low_v, values[mm], swapped[mm])
                            if e == 0
                            else jnp.where(low_v, swapped[mm], values[mm])
                        ).astype(BF16),
                        ones,
                    ],
                    axis=1,
                )
                for mm, e in tags
            }
            scores = {
                (mm, e): nt_dot(qbt[e * 4 * LAT : (e + 1) * 4 * LAT, :], keys[mm]).reshape(4, LAT, CB)
                + bias[...][None]
                for mm, e in tags
            }
            peaks = {t: jnp.max(scores[t], axis=-1, keepdims=True) for t in tags}
            weights = {t: jnp.exp(scores[t] - peaks[t]).astype(BF16) for t in tags}
            for mm, e in tags:
                sums = jnp.dot(
                    weights[mm, e].reshape(4 * LAT, CB), both[mm, e], preferred_element_type=F32
                )
                for t in range(2):
                    a = sums[2 * t * LAT : (2 * t + 1) * LAT]
                    b = sums[(2 * t + 1) * LAT : (2 * t + 2) * LAT]
                    top = jnp.where(low, a[:, :CB], b[:, :CB])
                    bottom = jnp.where(low, a[:, CB:], b[:, CB:])
                    lanes = (e * 2 + t) * CB
                    att[pair * n + mm, :, lanes : lanes + CB] = (top / bottom).astype(BF16)
            return 0

        lax.fori_loop(0, STEP // n, some, 0)
        mixed = jnp.dot(
            att[...].reshape(STEP * LAT, D), w_out[...], preferred_element_type=F32
        ).reshape(STEP, LAT, D)
        latents = (q[...].astype(F32)[None] + mixed).reshape(STEP, CHAN, LG, D)
        for g in range(CHAN):
            lsend[g, c * STEP : (c + 1) * STEP] = latents[:, g].astype(BF16)
        for i, o in enumerate(OFFSETS):
            lat_copy(o, i, c).start()
        own_copy(c).start()

    for c in range(CHUNKS):
        if c % 2 == 0:
            for i in reversed(range(len(OFFSETS))):
                o = OFFSETS[i]
                kv_copy(o, i, c // 2).wait_recv()
                spread(kv_recv, from_peer(o), c // 2)
        attend(c, 2)
        if c >= 2:
            forward(c - 2)
    for c in range(CHUNKS - 2, CHUNKS):
        forward(c)

    def regrid(source, l):
        for f in range(FT):
            turn[l, f, 0 : SCAN * LG] = source[:, :, f * CB : (f + 1) * CB].reshape(SCAN * LG, CB)
        for i in range(LG):
            for f in range(FT):
                grid_f[0, l, i, f, 8 : 8 + WIDE] = turn[l, f, pl.ds(i, WIDE, stride=LG), :]

    for c in range(CHUNKS):
        for s in range(2, CHAN - 2):
            await_latents(s, c)
    for l in range(LINES):
        regrid(lrecv[l].reshape(SCAN, LG, D).astype(F32), l + 1)

    def halo_copy(c, half, way):
        return pltpu.make_async_remote_copy(
            src_ref=hsend.at[c, half, way],
            dst_ref=hrecv.at[c, half, way],
            send_sem=h_ssem.at[c, half, way],
            recv_sem=h_rsem.at[c, half, way],
            device_id=(ways[way], me),
            device_id_type=MESH,
        )

    beyond = (tracks - 1, 0)
    edge_line = (LINES + 1, 0)

    def out_copy(l):
        return pltpu.make_async_copy(outb.at[l], out_h.at[l], out_sem.at[l])

    for c in range(LAYERS):
        now, later = c % 2, (c + 1) % 2
        final = c == LAYERS - 1

        def clear_pair(half, first, apart):
            def line(n, _):
                l = first + n * apart
                for f in range(FT):
                    for t in range(WIDE // 8):
                        cs = [coef[c, l, f, k, 8 * t : 8 * t + 8] for k in range(9)]
                        for i in range(HALF):
                            total = None
                            for k in range(9):
                                term = cs[k] * grid_f[
                                    now, l + k // 3, half * HALF + i, f, pl.ds(7 + 8 * t + k % 3, 8), :
                                ]
                                total = term if total is None else total + term
                            st[n, i, 8 * t : 8 * t + 8, f * CB : (f + 1) * CB] = total.astype(BF16)
                return 0

            lax.fori_loop(0, 2, line, 0)
            update = jnp.dot(
                st[...].reshape(2 * HALF * WIDE, D), w_mix[c], preferred_element_type=F32
            ).reshape(2, HALF, WIDE, D)
            for n in range(2):
                l = first + n * apart
                for i in range(HALF):
                    for f in range(FT):
                        lanes = slice(f * CB, (f + 1) * CB)
                        centre = grid_f[now, l + 1, half * HALF + i, f, 8 : 8 + WIDE]
                        cleared = (centre + update[n, i, :, lanes]).astype(BF16)
                        if final:
                            at = (half * HALF + i) * WIDE
                            last[l, f, at : at + WIDE] = cleared.astype(F32)
                        else:
                            grid_f[later, l + 1, half * HALF + i, f, 8 : 8 + WIDE] = cleared.astype(F32)
                            if apart > 1:
                                hsend[c, half, n, i, :, lanes] = cleared

        def finish_pair(first, apart):
            def column(p, _):
                for n in range(2):
                    for f in range(FT):
                        rows = last[first + n * apart, f, pl.ds(p, LG, stride=WIDE), :]
                        outb[first + n * apart, p, :, f * CB : (f + 1) * CB] = rows.astype(BF16)
                return 0

            lax.fori_loop(0, SCAN, column, 0)
            for n in range(2):
                out_copy(first + n * apart).start()

        for half in range(2):
            clear_pair(half, 1, 1)
        if final:
            finish_pair(1, 1)
        for half in range(2):
            for way in range(2):
                if c == 0:
                    if half == 0:
                        for n in range(CHUNKS):
                            near_copy(n, way).wait_recv()
                        beside = near[way].reshape(SCAN, LG, D).astype(F32)
                        regrid(jnp.where(track == beyond[way], 0.0, beside), edge_line[way])
                else:
                    halo_copy(c - 1, half, way).wait_recv()
                    for i in range(HALF):
                        for f in range(FT):
                            beside = hrecv[c - 1, half, way, i, :, f * CB : (f + 1) * CB].astype(F32)
                            grid_f[now, edge_line[way], half * HALF + i, f, 8 : 8 + WIDE] = jnp.where(
                                track == beyond[way], 0.0, beside
                            )
            clear_pair(half, 0, LINES - 1)
            if not final:
                for way in range(2):
                    halo_copy(c, half, way).start()
    finish_pair(0, LINES - 1)

    for i, o in enumerate(OFFSETS):
        for c in range(2):
            kv_copy(o, i, c).wait_send()
        for c in range(CHUNKS):
            lat_copy(o, i, c).wait_send()
    for way in range(2):
        for c in range(CHUNKS):
            near_copy(c, way).wait_send()
        for c in range(LAYERS - 1):
            for half in range(2):
                halo_copy(c, half, way).wait_send()
    for l in range(LINES):
        out_copy(l).wait()


def local(tracks, radiance, w_key, w_value, latent_query, band_blocks, band_count, valid_mask, w_out, conv_taps, w_mix):
    hbm = pl.BlockSpec(memory_space=pl.ANY)
    vmem = pltpu.VMEM
    dma = pltpu.SemaphoreType.DMA
    peers = len(OFFSETS)
    return pl.pallas_call(
        functools.partial(kernel, tracks),
        out_shape=jax.ShapeDtypeStruct((LINES, SCAN, LG, D), BF16),
        in_specs=[hbm] * 10,
        out_specs=hbm,
        scratch_shapes=[
            vmem((SCAN, BLK, LINES, CB), BF16),
            vmem((BLK, CB, CB), BF16),
            vmem((BLK, CB, CB), BF16),
            vmem((LAT, D), BF16),
            vmem((CHAN, MAXB), jnp.int32),
            pltpu.SMEM((CHAN,), jnp.int32),
            vmem((9, LINES, SCAN), jnp.int32),
            vmem((D, D), BF16),
            vmem((9, LAYERS, D), F32),
            vmem((LAYERS, D, D), BF16),
            vmem((SCAN * BLK * LINES + 72, CB), F32),
            vmem((CHAN, 2, 2, BLK, 8, CB), BF16),
            vmem((CHAN, 2, 2, BLK, 8, CB), BF16),
            vmem((2, CB * 8, CB), F32),
            vmem((2, CB * 8, CB), F32),
            vmem((HEADS * LAT, CB), BF16),
            vmem((LAT, CB), F32),
            vmem((STEP, LAT, D), BF16),
            vmem((CHAN, ROWS, LG, D), BF16),
            vmem((LINES, PER, 2, LG, D), BF16),
            vmem((2, PER, 2, LG, D), BF16),
            vmem((CB, CB), F32),
            vmem((LINES, 9, WIDE, CB), F32),
            vmem((LAYERS, LINES, FT, 9, WIDE, CB), F32),
            vmem((LINES + 2, FT, WIDE * LG, CB), F32),
            vmem((2, LINES + 2, LG, FT, WIDE + 16, CB), F32),
            vmem((2, HALF, WIDE, D), BF16),
            vmem((LAYERS - 1, 2, 2, HALF, WIDE, D), BF16),
            vmem((LAYERS - 1, 2, 2, HALF, WIDE, D), BF16),
            vmem((LINES, FT, LG * WIDE, CB), F32),
            vmem((LINES, SCAN, LG, D), BF16),
            dma((10,)),
            dma((2, peers)), dma((2, peers)),
            dma((CHUNKS, peers)), dma((CHUNKS, CHAN)),
            dma((CHUNKS, 2)), dma((CHUNKS, 2)),
            dma((LAYERS - 1, 2, 2)), dma((LAYERS - 1, 2, 2)),
            dma((LINES,)),
        ],
        compiler_params=pltpu.CompilerParams(
            collective_id=0, has_side_effects=True, vmem_limit_bytes=60 * 1024 * 1024
        ),
    )(
        jnp.transpose(radiance, (1, 2, 0, 3)), w_key, w_value, latent_query, band_blocks, band_count,
        jnp.transpose(valid_mask, (2, 0, 1)), w_out, jnp.transpose(conv_taps, (1, 0, 2)), w_mix,
    )


def solution(mesh):
    return jax.shard_map(
        functools.partial(local, mesh.shape["track"]),
        mesh=mesh,
        in_specs=(
            P("track", None, "chan", None),
            P("chan", None, None),
            P("chan", None, None),
            P(),
            P(),
            P(),
            P("track", None, None),
            P(),
            P(),
            P(),
        ),
        out_specs=P("track", None, "chan", None),
        check_vma=False,
    )
```

```python
import functools

import jax
import jax.numpy as jnp
from jax import lax
from jax.experimental import pallas as pl
from jax.experimental.pallas import tpu as pltpu
from jax.sharding import PartitionSpec as P

HEADS = 8
HEAD_DIM = 64
NBLK = 72
LAYERS = 3
DEEP = 2
NX, NY = 4, 2
CHAN = NX * NY
LINES, SCAN = 4, 30
WIDE = 32
PER = LINES * SCAN // CHAN
ROWS = 16
BLK = NBLK // CHAN
LAT, D, CB = 64, 512, 128
FT = D // CB
LG = LAT // CHAN
MAXB = 48
HALF = LG // 2
STEP = 4
CHUNKS = ROWS // STEP
EXCH = max(LAYERS - DEEP, 1)
ALL = LINES + 2 * DEEP
CLEAR = ALL - 2
MASKED = -1e30
MESH = pl.DeviceIdType.MESH
OFFSETS = ((2, 1), (2, 0), (1, 1), (3, 1), (1, 0), (3, 0), (0, 1))
BF16, F32 = jnp.bfloat16, jnp.float32


def nt_dot(a, b):
    return lax.dot_general(a, b, (((1,), (1,)), ((), ())), preferred_element_type=F32)


def chunk_at(c):
    return pl.ds(c * STEP, min(STEP, PER - c * STEP))


def kernel(
    tracks, rad_h, wk_h, wv_h, q_h, bb_h, cnt_h, vm_h, w_out_h, taps_h, w_mix_h, out_h,
    rad, wk, wv, q, bb, cnt, vm, w_out, taps, w_mix, vm_near,
    xf, kv_send, kv_recv, kf, vf, qbt, bias, att, lsend, lrecv, near,
    vmf, mb, coef, turn, grid_f, st, hsend, hrecv, last, outb,
    in_sem, kv_ssem, kv_rsem, l_ssem, l_rsem, n_ssem, n_rsem, v_ssem, v_rsem, h_ssem, h_rsem, out_sem,
):
    track, me = lax.axis_index("track"), lax.axis_index("chan")
    x, y = me // NY, me % NY
    up, down = (track + tracks - 1) % tracks, (track + 1) % tracks
    ways = (up, down)
    not_first, not_last = track > 0, track < tracks - 1
    sends, comes = (not_first, not_last), (not_last, not_first)

    def to_peer(o):
        return ((x + o[0]) % NX) * NY + (y + o[1]) % NY

    def from_peer(o):
        return ((x + NX - o[0]) % NX) * NY + (y + NY - o[1]) % NY

    barrier = pltpu.get_barrier_semaphore()
    for o in OFFSETS:
        pl.semaphore_signal(barrier, inc=1, device_id=(track, to_peer(o)), device_id_type=MESH)
    for way in range(2):

        @pl.when(sends[way])
        def _():
            pl.semaphore_signal(barrier, inc=1, device_id=(ways[way], me), device_id_type=MESH)

    loads = [
        pltpu.make_async_copy(src, dst, in_sem.at[i])
        for i, (src, dst) in enumerate(
            (
                (rad_h, rad), (wk_h, wk), (wv_h, wv), (q_h, q), (bb_h, bb), (cnt_h, cnt),
                (vm_h, vm), (taps_h, taps), (w_out_h, w_out), (w_mix_h, w_mix),
            )
        )
    ]
    for load in loads:
        load.start()

    xf[pl.ds(SCAN * BLK * LINES, 72), :] = jnp.zeros((72, CB), F32)
    loads[0].wait()
    xf[pl.ds(0, SCAN * BLK * LINES), :] = rad[...].astype(F32).reshape(SCAN * BLK * LINES, CB)
    loads[1].wait()
    loads[2].wait()

    for b in range(BLK):
        rows = jnp.concatenate(
            [
                xf[pl.ds((j % 2) * BLK * LINES + b * LINES + j // 2, ROWS, stride=2 * BLK * LINES), :]
                for j in range(CHAN)
            ],
            axis=0,
        )
        inverse = lax.rsqrt(jnp.mean(rows * rows, axis=-1, keepdims=True) + 1e-05)
        normed = (rows * inverse).astype(BF16)
        keys = jnp.dot(rows.astype(BF16), wk[b], preferred_element_type=F32)
        values = jnp.dot(normed, wv[b], preferred_element_type=F32)
        kv_send[:, :, 0, b] = keys.astype(BF16).reshape(CHAN, 2, 8, CB)
        kv_send[:, :, 1, b] = values.astype(BF16).reshape(CHAN, 2, 8, CB)

    pl.semaphore_wait(barrier, len(OFFSETS) + not_first.astype(jnp.int32) + not_last.astype(jnp.int32))

    def kv_copy(o, i, c):
        return pltpu.make_async_remote_copy(
            src_ref=kv_send.at[to_peer(o), c],
            dst_ref=kv_recv.at[me, c],
            send_sem=kv_ssem.at[c, i],
            recv_sem=kv_rsem.at[c, i],
            device_id=(track, to_peer(o)),
            device_id_type=MESH,
        )

    for c in range(2):
        for i, o in enumerate(OFFSETS):
            kv_copy(o, i, c).start()

    for load in loads[3:]:
        load.wait()

    def vm_copy(way):
        return pltpu.make_async_remote_copy(
            src_ref=vm,
            dst_ref=vm_near.at[way],
            send_sem=v_ssem.at[way],
            recv_sem=v_rsem.at[way],
            device_id=(ways[way], me),
            device_id_type=MESH,
        )

    for way in range(2):

        @pl.when(sends[way])
        def _():
            vm_copy(way).start()

    lane = lax.broadcasted_iota(jnp.int32, (LAT, CB), 1)
    low = lane < HEAD_DIM
    for h in range(HEADS):
        e = h // 4
        part = q[:, (h // 2) * CB : (h // 2 + 1) * CB].astype(F32) * HEAD_DIM**-0.5
        if h % 2 != e:
            part = pltpu.roll(part, HEAD_DIM, 1)
        part = jnp.where(low if e == 0 else jnp.logical_not(low), part, 0.0)
        qbt[h * LAT : (h + 1) * LAT, :] = part.astype(BF16)

    group = lax.broadcasted_iota(jnp.int32, (CHAN, MAXB), 0)
    slot = lax.broadcasted_iota(jnp.int32, (CHAN, MAXB), 1)
    used = jnp.zeros((CHAN, MAXB), jnp.int32)
    for g in range(CHAN):
        used = jnp.where(group == g, cnt[g], used)
    blocks = jnp.where(slot < used, bb[...], -1)
    block_of = lax.broadcasted_iota(jnp.int32, (CHAN, CB), 1)
    allowed = jnp.full((CHAN, CB), MASKED, F32)
    for j in range(MAXB):
        allowed = jnp.where(blocks[:, j : j + 1] == block_of, 0.0, allowed)
    for g in range(CHAN):
        bias[g * LG : (g + 1) * LG, :] = jnp.broadcast_to(allowed[g : g + 1], (LG, CB))

    kf[:, pl.ds(NBLK * 8, (CB - NBLK) * 8), :] = jnp.zeros((2, (CB - NBLK) * 8, CB), F32)
    vf[:, pl.ds(NBLK * 8, (CB - NBLK) * 8), :] = jnp.zeros((2, (CB - NBLK) * 8, CB), F32)

    def spread(ref, s, c):
        at = pl.ds(pl.multiple_of(s * (BLK * 8), BLK * 8), BLK * 8)
        kf[c, at, :] = ref[s, c, 0].astype(F32).reshape(BLK * 8, CB)
        vf[c, at, :] = ref[s, c, 1].astype(F32).reshape(BLK * 8, CB)

    for c in range(2):
        spread(kv_send, me, c)

    def validity(slot, source, lines):
        vmf[slot] = jnp.zeros((CB, CB), F32)
        for k in range(9):
            vmf[slot, k * LINES : (k + 1) * LINES, 0:SCAN] = source(k).astype(F32)
        turned = vmf[slot].T
        for l, to in lines:
            for k in range(9):
                col = turned[:WIDE, k * LINES + l : k * LINES + l + 1]
                mb[to, k] = jnp.broadcast_to(col, (WIDE, CB))

    validity(0, lambda k: vm[k], [(l, l + DEEP - 1) for l in range(LINES)])
    for way in range(2):

        @pl.when(comes[way])
        def _():
            vm_copy(way).wait_recv()

            if way == 0:
                lines = [(l, DEEP - 1 + LINES + l) for l in range(DEEP - 1)]
            else:
                lines = [(LINES - DEEP + 1 + l, l) for l in range(DEEP - 1)]
            validity(1 + way, lambda k: vm_near[way, k], lines)

        @pl.when(jnp.logical_not(comes[way]))
        def _():
            for l in range(DEEP - 1):
                mb[l if way == 1 else DEEP - 1 + LINES + l] = jnp.zeros((9, WIDE, CB), F32)

    def coefficients(l, _):
        for c in range(LAYERS):
            for f in range(FT):
                for k in range(9):
                    coef[c, l, f, k] = mb[l, k] * taps[k, c : c + 1, f * CB : (f + 1) * CB]
        return 0

    lax.fori_loop(0, CLEAR, coefficients, 0)

    def borders(l, _):
        for s in range(2):
            for i in range(LG):
                grid_f[s, l, i, :, 0:8] = jnp.zeros((FT, 8, CB), F32)
                grid_f[s, l, i, :, 8 + WIDE : 16 + WIDE] = jnp.zeros((FT, 8, CB), F32)
        turn[l, :, SCAN * LG : WIDE * LG] = jnp.zeros((FT, (WIDE - SCAN) * LG, CB), F32)
        return 0

    lax.fori_loop(0, ALL, borders, 0)

    line_me, side_me = me // 2, me % 2

    def lat_copy(o, i, c):
        return pltpu.make_async_remote_copy(
            src_ref=lsend.at[to_peer(o), chunk_at(c)],
            dst_ref=lrecv.at[line_me, chunk_at(c), side_me],
            send_sem=l_ssem.at[c, i],
            recv_sem=l_rsem.at[c, me],
            device_id=(track, to_peer(o)),
            device_id_type=MESH,
        )

    def own_copy(c):
        return pltpu.make_async_copy(
            lsend.at[me, chunk_at(c)],
            lrecv.at[line_me, chunk_at(c), side_me],
            l_rsem.at[c, me],
        )

    def await_latents(s, c):
        pltpu.make_async_copy(
            lsend.at[s, chunk_at(c)], lrecv.at[s // 2, chunk_at(c), s % 2], l_rsem.at[c, s]
        ).wait()

    def near_copy(c, way):
        return pltpu.make_async_remote_copy(
            src_ref=lrecv.at[pl.ds(way * (LINES - DEEP), DEEP), chunk_at(c)],
            dst_ref=near.at[way, :, chunk_at(c)],
            send_sem=n_ssem.at[c, way],
            recv_sem=n_rsem.at[c, way],
            device_id=(ways[way], me),
            device_id_type=MESH,
        )

    def forward(c):
        for s in range(CHAN):
            if s // 2 < DEEP or s // 2 >= LINES - DEEP:
                await_latents(s, c)
        for way in range(2):

            @pl.when(sends[way])
            def _():
                near_copy(c, way).start()

    ones = jnp.ones((CB, CB), BF16)
    low_v = lax.broadcasted_iota(jnp.int32, (CB, CB), 1) < HEAD_DIM

    def attend(c, n):
        def some(pair, _):
            tags = [(mm, e) for mm in range(n) for e in range(2)]
            at = [c % 2 * STEP + pair * n + mm for mm in range(n)]
            keys = [kf[c // 2, pl.ds(a, CB, stride=8), :].astype(BF16) for a in at]
            values = [vf[c // 2, pl.ds(a, CB, stride=8), :] for a in at]
            swapped = [pltpu.roll(v, HEAD_DIM, 1) for v in values]
            both = {
                (mm, e): jnp.concatenate(
                    [
                        (
                            jnp.where(low_v, values[mm], swapped[mm])
                            if e == 0
                            else jnp.where(low_v, swapped[mm], values[mm])
                        ).astype(BF16),
                        ones,
                    ],
                    axis=1,
                )
                for mm, e in tags
            }
            scores = {
                (mm, e): nt_dot(qbt[e * 4 * LAT : (e + 1) * 4 * LAT, :], keys[mm]).reshape(4, LAT, CB)
                + bias[...][None]
                for mm, e in tags
            }
            peaks = {t: jnp.max(scores[t], axis=-1, keepdims=True) for t in tags}
            weights = {t: jnp.exp(scores[t] - peaks[t]).astype(BF16) for t in tags}
            for mm, e in tags:
                sums = jnp.dot(
                    weights[mm, e].reshape(4 * LAT, CB), both[mm, e], preferred_element_type=F32
                )
                for t in range(2):
                    a = sums[2 * t * LAT : (2 * t + 1) * LAT]
                    b = sums[(2 * t + 1) * LAT : (2 * t + 2) * LAT]
                    top = jnp.where(low, a[:, :CB], b[:, :CB])
                    bottom = jnp.where(low, a[:, CB:], b[:, CB:])
                    lanes = (e * 2 + t) * CB
                    att[pair * n + mm, :, lanes : lanes + CB] = (top / bottom).astype(BF16)
            return 0

        lax.fori_loop(0, STEP // n, some, 0)
        mixed = jnp.dot(
            att[...].reshape(STEP * LAT, D), w_out[...], preferred_element_type=F32
        ).reshape(STEP, LAT, D)
        latents = (q[...].astype(F32)[None] + mixed).reshape(STEP, CHAN, LG, D)
        for g in range(CHAN):
            lsend[g, c * STEP : (c + 1) * STEP] = latents[:, g].astype(BF16)
        for i, o in enumerate(OFFSETS):
            lat_copy(o, i, c).start()
        own_copy(c).start()

    for c in range(CHUNKS):
        if c % 2 == 0:
            for i in reversed(range(len(OFFSETS))):
                o = OFFSETS[i]
                kv_copy(o, i, c // 2).wait_recv()
                spread(kv_recv, from_peer(o), c // 2)
        attend(c, 2)
        if c >= 2:
            forward(c - 2)
    for c in range(CHUNKS - 2, CHUNKS):
        forward(c)

    def regrid(source, l):
        for f in range(FT):
            turn[l, f, 0 : SCAN * LG] = source[:, :, f * CB : (f + 1) * CB].reshape(SCAN * LG, CB)
        for i in range(LG):
            for f in range(FT):
                grid_f[0, l, i, f, 8 : 8 + WIDE] = turn[l, f, pl.ds(i, WIDE, stride=LG), :]

    for c in range(CHUNKS):
        for s in range(CHAN):
            if not (s // 2 < DEEP or s // 2 >= LINES - DEEP):
                await_latents(s, c)
    for l in range(LINES):
        regrid(lrecv[l].reshape(SCAN, LG, D).astype(F32), l + DEEP)

    def halo_copy(c, half, way):
        return pltpu.make_async_remote_copy(
            src_ref=hsend.at[c - DEEP, half, way],
            dst_ref=hrecv.at[c - DEEP, half, way],
            send_sem=h_ssem.at[c - DEEP, half, way],
            recv_sem=h_rsem.at[c - DEEP, half, way],
            device_id=(ways[way], me),
            device_id_type=MESH,
        )

    def out_copy(l):
        return pltpu.make_async_copy(outb.at[l], out_h.at[l], out_sem.at[l])

    def clear_pair(c, half, out):
        now, later = c % 2, (c + 1) % 2
        apart = CLEAR - 1 - 2 * out
        own = out - DEEP + 1
        final = c == LAYERS - 1

        def line(n, _):
            l = out + n * apart
            for f in range(FT):
                for t in range(WIDE // 8):
                    cs = [coef[c, l, f, k, 8 * t : 8 * t + 8] for k in range(9)]
                    for i in range(HALF):
                        total = None
                        for k in range(9):
                            term = cs[k] * grid_f[
                                now, l + k // 3, half * HALF + i, f, pl.ds(7 + 8 * t + k % 3, 8), :
                            ]
                            total = term if total is None else total + term
                        st[n, i, 8 * t : 8 * t + 8, f * CB : (f + 1) * CB] = total.astype(BF16)
            return 0

        lax.fori_loop(0, 2, line, 0)
        update = jnp.dot(
            st[...].reshape(2 * HALF * WIDE, D), w_mix[c], preferred_element_type=F32
        ).reshape(2, HALF, WIDE, D)
        for n in range(2):
            l = out + n * apart
            for i in range(HALF):
                for f in range(FT):
                    lanes = slice(f * CB, (f + 1) * CB)
                    centre = grid_f[now, l + 1, half * HALF + i, f, 8 : 8 + WIDE]
                    cleared = (centre + update[n, i, :, lanes]).astype(BF16)
                    wide = cleared.astype(F32)
                    if final:
                        at = (half * HALF + i) * WIDE
                        last[l - DEEP + 1, f, at : at + WIDE] = wide
                    else:
                        if own < 0:
                            wide = jnp.where(comes[1 - n], wide, 0.0)
                        grid_f[later, l + 1, half * HALF + i, f, 8 : 8 + WIDE] = wide
                        if own == 0 and c + 1 >= DEEP:
                            hsend[c + 1 - DEEP, half, n, i, :, lanes] = cleared
        if own == 0 and not final and c + 1 >= DEEP:
            for way in range(2):

                @pl.when(sends[way])
                def _():
                    halo_copy(c + 1, half, way).start()

    def finish_pair(first, apart):
        def column(p, _):
            for n in range(2):
                for f in range(FT):
                    rows = last[first + n * apart, f, pl.ds(p, LG, stride=WIDE), :]
                    outb[first + n * apart, p, :, f * CB : (f + 1) * CB] = rows.astype(BF16)
            return 0

        lax.fori_loop(0, SCAN, column, 0)
        for n in range(2):
            out_copy(first + n * apart).start()

    def take_near():
        for way in range(2):
            base = (DEEP + LINES, 0)[way]

            @pl.when(comes[way])
            def _():
                for n in range(CHUNKS):
                    near_copy(n, way).wait_recv()
                for d in range(DEEP):
                    regrid(near[way, d].reshape(SCAN, LG, D).astype(F32), base + d)

            @pl.when(jnp.logical_not(comes[way]))
            def _():
                for d in range(DEEP):
                    for i in range(LG):
                        grid_f[0, base + d, i, :, 8 : 8 + WIDE] = jnp.zeros((FT, WIDE, CB), F32)

    def take_halo(c, half, way):
        edge = (DEEP + LINES, DEEP - 1)[way]
        own = pl.ds(half * HALF, HALF)

        @pl.when(comes[way])
        def _():
            halo_copy(c, half, way).wait_recv()
            for f in range(FT):
                grid_f[c % 2, edge, own, f, 8 : 8 + WIDE] = hrecv[
                    c - DEEP, half, way, :, :, f * CB : (f + 1) * CB
                ].astype(F32)

        @pl.when(jnp.logical_not(comes[way]))
        def _():
            for f in range(FT):
                grid_f[c % 2, edge, own, f, 8 : 8 + WIDE] = jnp.zeros((HALF, WIDE, CB), F32)

    inner, outer = DEEP, DEEP - 1
    for half in range(2):
        clear_pair(0, half, inner)
    take_near()
    for out in range(outer, -1, -1):
        for half in range(2):
            clear_pair(0, half, out)
    for c in range(1, LAYERS):
        if c < DEEP:
            for out in range(c, DEEP + 1):
                for half in range(2):
                    clear_pair(c, half, out)
                if out == inner and c == LAYERS - 1:
                    finish_pair(1, 1)
        else:
            for half in range(2):
                clear_pair(c, half, inner)
            if c == LAYERS - 1:
                finish_pair(1, 1)
            for half in range(2):
                for way in range(2):
                    take_halo(c, half, way)
                clear_pair(c, half, outer)
    finish_pair(0, LINES - 1)

    for i, o in enumerate(OFFSETS):
        for c in range(2):
            kv_copy(o, i, c).wait_send()
        for c in range(CHUNKS):
            lat_copy(o, i, c).wait_send()
    for way in range(2):

        @pl.when(sends[way])
        def _():
            vm_copy(way).wait_send()
            for c in range(CHUNKS):
                near_copy(c, way).wait_send()
            for c in range(DEEP, LAYERS):
                for half in range(2):
                    halo_copy(c, half, way).wait_send()

    for l in range(LINES):
        out_copy(l).wait()


def local(tracks, radiance, w_key, w_value, latent_query, band_blocks, band_count, valid_mask, w_out, conv_taps, w_mix):
    hbm = pl.BlockSpec(memory_space=pl.ANY)
    vmem = pltpu.VMEM
    dma = pltpu.SemaphoreType.DMA
    peers = len(OFFSETS)
    return pl.pallas_call(
        functools.partial(kernel, tracks),
        out_shape=jax.ShapeDtypeStruct((LINES, SCAN, LG, D), BF16),
        in_specs=[hbm] * 10,
        out_specs=hbm,
        scratch_shapes=[
            vmem((SCAN, BLK, LINES, CB), BF16),
            vmem((BLK, CB, CB), BF16),
            vmem((BLK, CB, CB), BF16),
            vmem((LAT, D), BF16),
            vmem((CHAN, MAXB), jnp.int32),
            pltpu.SMEM((CHAN,), jnp.int32),
            vmem((9, LINES, SCAN), jnp.int32),
            vmem((D, D), BF16),
            vmem((9, LAYERS, D), F32),
            vmem((LAYERS, D, D), BF16),
            vmem((2, 9, LINES, SCAN), jnp.int32),
            vmem((SCAN * BLK * LINES + 72, CB), F32),
            vmem((CHAN, 2, 2, BLK, 8, CB), BF16),
            vmem((CHAN, 2, 2, BLK, 8, CB), BF16),
            vmem((2, CB * 8, CB), F32),
            vmem((2, CB * 8, CB), F32),
            vmem((HEADS * LAT, CB), BF16),
            vmem((LAT, CB), F32),
            vmem((STEP, LAT, D), BF16),
            vmem((CHAN, ROWS, LG, D), BF16),
            vmem((LINES, PER, 2, LG, D), BF16),
            vmem((2, DEEP, PER, 2, LG, D), BF16),
            vmem((3, CB, CB), F32),
            vmem((CLEAR, 9, WIDE, CB), F32),
            vmem((LAYERS, CLEAR, FT, 9, WIDE, CB), F32),
            vmem((ALL, FT, WIDE * LG, CB), F32),
            vmem((2, ALL, LG, FT, WIDE + 16, CB), F32),
            vmem((2, HALF, WIDE, D), BF16),
            vmem((EXCH, 2, 2, HALF, WIDE, D), BF16),
            vmem((EXCH, 2, 2, HALF, WIDE, D), BF16),
            vmem((LINES, FT, LG * WIDE, CB), F32),
            vmem((LINES, SCAN, LG, D), BF16),
            dma((10,)),
            dma((2, peers)), dma((2, peers)),
            dma((CHUNKS, peers)), dma((CHUNKS, CHAN)),
            dma((CHUNKS, 2)), dma((CHUNKS, 2)),
            dma((2,)), dma((2,)),
            dma((EXCH, 2, 2)), dma((EXCH, 2, 2)),
            dma((LINES,)),
        ],
        compiler_params=pltpu.CompilerParams(
            collective_id=0, has_side_effects=True, vmem_limit_bytes=60 * 1024 * 1024
        ),
    )(
        jnp.transpose(radiance, (1, 2, 0, 3)), w_key, w_value, latent_query, band_blocks, band_count,
        jnp.transpose(valid_mask, (2, 0, 1)), w_out, jnp.transpose(conv_taps, (1, 0, 2)), w_mix,
    )


def solution(mesh):
    return jax.shard_map(
        functools.partial(local, mesh.shape["track"]),
        mesh=mesh,
        in_specs=(
            P("track", None, "chan", None),
            P("chan", None, None),
            P("chan", None, None),
            P(),
            P(),
            P(),
            P("track", None, None),
            P(),
            P(),
            P(),
        ),
        out_specs=P("track", None, "chan", None),
        check_vma=False,
    )
```

```python
import functools

import jax
import jax.numpy as jnp
from jax import lax
from jax.experimental import pallas as pl
from jax.experimental.pallas import tpu as pltpu
from jax.sharding import PartitionSpec as P

HEADS = 8
HEAD_DIM = 64
NBLK = 72
LAYERS = 3
DEEP = 2
NX, NY = 4, 2
CHAN = NX * NY
LINES, SCAN = 4, 30
WIDE = 32
PER = LINES * SCAN // CHAN
ROWS = 16
BLK = NBLK // CHAN
LAT, D, CB = 64, 512, 128
FT = D // CB
LG = LAT // CHAN
MAXB = 48
HALF = LG // 2
STEP = 4
CHUNKS = ROWS // STEP
EXCH = max(LAYERS - DEEP, 1)
ALL = LINES + 2 * DEEP
CLEAR = ALL - 2
MASKED = -1e30
MESH = pl.DeviceIdType.MESH
OFFSETS = ((2, 1), (2, 0), (1, 1), (3, 1), (1, 0), (3, 0), (0, 1))
BF16, F32 = jnp.bfloat16, jnp.float32


def nt_dot(a, b):
    return lax.dot_general(a, b, (((1,), (1,)), ((), ())), preferred_element_type=F32)


def chunk_at(c):
    return pl.ds(c * STEP, min(STEP, PER - c * STEP))


def kernel(
    tracks, rad_h, wk_h, wv_h, q_h, bb_h, cnt_h, vm_h, w_out_h, taps_h, w_mix_h, out_h,
    rad, wk, wv, q, bb, cnt, vm, w_out, taps, w_mix, vm_near,
    xf, kv_send, kv_recv, kf, vf, qbt, bias, att, lsend, lrecv, near,
    vmf, mb, coef, turn, grid_f, st, hsend, hrecv, last, outb,
    in_sem, kv_ssem, kv_rsem, l_ssem, l_rsem, n_ssem, n_rsem, v_ssem, v_rsem, h_ssem, h_rsem, out_sem,
):
    track, me = lax.axis_index("track"), lax.axis_index("chan")
    x, y = me // NY, me % NY
    up, down = (track + tracks - 1) % tracks, (track + 1) % tracks
    ways = (up, down)
    not_first, not_last = track > 0, track < tracks - 1
    sends, comes = (not_first, not_last), (not_last, not_first)

    def to_peer(o):
        return ((x + o[0]) % NX) * NY + (y + o[1]) % NY

    def from_peer(o):
        return ((x + NX - o[0]) % NX) * NY + (y + NY - o[1]) % NY

    barrier = pltpu.get_barrier_semaphore()
    for o in OFFSETS:
        pl.semaphore_signal(barrier, inc=1, device_id=(track, to_peer(o)), device_id_type=MESH)
    for way in range(2):

        @pl.when(sends[way])
        def _():
            pl.semaphore_signal(barrier, inc=1, device_id=(ways[way], me), device_id_type=MESH)

    loads = [
        pltpu.make_async_copy(src, dst, in_sem.at[i])
        for i, (src, dst) in enumerate(
            (
                (rad_h, rad), (wk_h, wk), (wv_h, wv), (q_h, q), (bb_h, bb), (cnt_h, cnt),
                (vm_h, vm), (taps_h, taps), (w_out_h, w_out), (w_mix_h, w_mix),
            )
        )
    ]
    for load in loads:
        load.start()

    xf[pl.ds(SCAN * BLK * LINES, 72), :] = jnp.zeros((72, CB), F32)
    loads[0].wait()
    xf[pl.ds(0, SCAN * BLK * LINES), :] = rad[...].astype(F32).reshape(SCAN * BLK * LINES, CB)
    loads[1].wait()
    loads[2].wait()

    for b in range(BLK):
        rows = jnp.concatenate(
            [
                xf[pl.ds((j % 2) * PER * BLK * LINES + b * LINES + j // 2, ROWS, stride=BLK * LINES), :]
                for j in range(CHAN)
            ],
            axis=0,
        )
        inverse = lax.rsqrt(jnp.mean(rows * rows, axis=-1, keepdims=True) + 1e-05)
        normed = (rows * inverse).astype(BF16)
        keys = jnp.dot(rows.astype(BF16), wk[b], preferred_element_type=F32)
        values = jnp.dot(normed, wv[b], preferred_element_type=F32)
        kv_send[:, :, 0, b] = keys.astype(BF16).reshape(CHAN, CHUNKS, STEP, CB)
        kv_send[:, :, 1, b] = values.astype(BF16).reshape(CHAN, CHUNKS, STEP, CB)

    pl.semaphore_wait(barrier, len(OFFSETS) + not_first.astype(jnp.int32) + not_last.astype(jnp.int32))

    def kv_copy(o, i, c):
        return pltpu.make_async_remote_copy(
            src_ref=kv_send.at[to_peer(o), c],
            dst_ref=kv_recv.at[me, c],
            send_sem=kv_ssem.at[c, i],
            recv_sem=kv_rsem.at[c, i],
            device_id=(track, to_peer(o)),
            device_id_type=MESH,
        )

    for c in range(CHUNKS):
        for i, o in enumerate(OFFSETS):
            kv_copy(o, i, c).start()

    for load in loads[3:]:
        load.wait()

    def vm_copy(way):
        return pltpu.make_async_remote_copy(
            src_ref=vm,
            dst_ref=vm_near.at[way],
            send_sem=v_ssem.at[way],
            recv_sem=v_rsem.at[way],
            device_id=(ways[way], me),
            device_id_type=MESH,
        )

    for way in range(2):

        @pl.when(sends[way])
        def _():
            vm_copy(way).start()

    lane = lax.broadcasted_iota(jnp.int32, (LAT, CB), 1)
    low = lane < HEAD_DIM
    for h in range(HEADS):
        e = h // 4
        part = q[:, (h // 2) * CB : (h // 2 + 1) * CB].astype(F32) * HEAD_DIM**-0.5
        if h % 2 != e:
            part = pltpu.roll(part, HEAD_DIM, 1)
        part = jnp.where(low if e == 0 else jnp.logical_not(low), part, 0.0)
        qbt[h * LAT : (h + 1) * LAT, :] = part.astype(BF16)

    group = lax.broadcasted_iota(jnp.int32, (CHAN, MAXB), 0)
    slot = lax.broadcasted_iota(jnp.int32, (CHAN, MAXB), 1)
    used = jnp.zeros((CHAN, MAXB), jnp.int32)
    for g in range(CHAN):
        used = jnp.where(group == g, cnt[g], used)
    blocks = jnp.where(slot < used, bb[...], -1)
    block_of = lax.broadcasted_iota(jnp.int32, (CHAN, CB), 1)
    allowed = jnp.full((CHAN, CB), MASKED, F32)
    for j in range(MAXB):
        allowed = jnp.where(blocks[:, j : j + 1] == block_of, 0.0, allowed)
    for g in range(CHAN):
        bias[g * LG : (g + 1) * LG, :] = jnp.broadcast_to(allowed[g : g + 1], (LG, CB))

    kf[:, pl.ds(NBLK * STEP, (CB - NBLK) * STEP), :] = jnp.zeros((CHUNKS, (CB - NBLK) * STEP, CB), F32)
    vf[:, pl.ds(NBLK * STEP, (CB - NBLK) * STEP), :] = jnp.zeros((CHUNKS, (CB - NBLK) * STEP, CB), F32)

    def spread(ref, s, c):
        at = pl.ds(s * (BLK * STEP), BLK * STEP)
        kf[c, at, :] = ref[s, c, 0].astype(F32).reshape(BLK * STEP, CB)
        vf[c, at, :] = ref[s, c, 1].astype(F32).reshape(BLK * STEP, CB)

    for c in range(CHUNKS):
        spread(kv_send, me, c)

    def validity(slot, source, lines):
        vmf[slot] = jnp.zeros((CB, CB), F32)
        for k in range(9):
            vmf[slot, k * LINES : (k + 1) * LINES, 0:SCAN] = source(k).astype(F32)
        turned = vmf[slot].T
        for l, to in lines:
            for k in range(9):
                col = turned[:WIDE, k * LINES + l : k * LINES + l + 1]
                mb[to, k] = jnp.broadcast_to(col, (WIDE, CB))

    validity(0, lambda k: vm[k], [(l, l + DEEP - 1) for l in range(LINES)])
    for way in range(2):

        @pl.when(comes[way])
        def _():
            vm_copy(way).wait_recv()

            if way == 0:
                lines = [(l, DEEP - 1 + LINES + l) for l in range(DEEP - 1)]
            else:
                lines = [(LINES - DEEP + 1 + l, l) for l in range(DEEP - 1)]
            validity(1 + way, lambda k: vm_near[way, k], lines)

        @pl.when(jnp.logical_not(comes[way]))
        def _():
            for l in range(DEEP - 1):
                mb[l if way == 1 else DEEP - 1 + LINES + l] = jnp.zeros((9, WIDE, CB), F32)

    def coefficients(l, _):
        for c in range(LAYERS):
            for f in range(FT):
                for k in range(9):
                    coef[c, l, f, k] = mb[l, k] * taps[k, c : c + 1, f * CB : (f + 1) * CB]
        return 0

    lax.fori_loop(0, CLEAR, coefficients, 0)

    def borders(l, _):
        for s in range(2):
            for i in range(LG):
                grid_f[s, l, i, :, 0:8] = jnp.zeros((FT, 8, CB), F32)
                grid_f[s, l, i, :, 8 + WIDE : 16 + WIDE] = jnp.zeros((FT, 8, CB), F32)
        turn[l, :, SCAN * LG : WIDE * LG] = jnp.zeros((FT, (WIDE - SCAN) * LG, CB), F32)
        return 0

    lax.fori_loop(0, ALL, borders, 0)

    line_me, side_me = me // 2, me % 2

    def lat_copy(o, i, c):
        return pltpu.make_async_remote_copy(
            src_ref=lsend.at[to_peer(o), chunk_at(c)],
            dst_ref=lrecv.at[line_me, side_me, chunk_at(c)],
            send_sem=l_ssem.at[c, i],
            recv_sem=l_rsem.at[c, me],
            device_id=(track, to_peer(o)),
            device_id_type=MESH,
        )

    def own_copy(c):
        return pltpu.make_async_copy(
            lsend.at[me, chunk_at(c)],
            lrecv.at[line_me, side_me, chunk_at(c)],
            l_rsem.at[c, me],
        )

    def await_latents(s, c):
        pltpu.make_async_copy(
            lsend.at[s, chunk_at(c)], lrecv.at[s // 2, s % 2, chunk_at(c)], l_rsem.at[c, s]
        ).wait()

    def near_copy(c, way):
        return pltpu.make_async_remote_copy(
            src_ref=lrecv.at[pl.ds(way * (LINES - DEEP), DEEP), :, chunk_at(c)],
            dst_ref=near.at[way, :, :, chunk_at(c)],
            send_sem=n_ssem.at[c, way],
            recv_sem=n_rsem.at[c, way],
            device_id=(ways[way], me),
            device_id_type=MESH,
        )

    def forward(c):
        for s in range(CHAN):
            if s // 2 < DEEP or s // 2 >= LINES - DEEP:
                await_latents(s, c)
        for way in range(2):

            @pl.when(sends[way])
            def _():
                near_copy(c, way).start()

    ones = jnp.ones((CB, CB), BF16)
    low_v = lax.broadcasted_iota(jnp.int32, (CB, CB), 1) < HEAD_DIM

    def attend(c, n):
        def some(pair, _):
            tags = [(mm, e) for mm in range(n) for e in range(2)]
            at = [pair * n + mm for mm in range(n)]
            keys = [kf[c, pl.ds(a, CB, stride=STEP), :].astype(BF16) for a in at]
            values = [vf[c, pl.ds(a, CB, stride=STEP), :] for a in at]
            swapped = [pltpu.roll(v, HEAD_DIM, 1) for v in values]
            both = {
                (mm, e): jnp.concatenate(
                    [
                        (
                            jnp.where(low_v, values[mm], swapped[mm])
                            if e == 0
                            else jnp.where(low_v, swapped[mm], values[mm])
                        ).astype(BF16),
                        ones,
                    ],
                    axis=1,
                )
                for mm, e in tags
            }
            scores = {
                (mm, e): nt_dot(qbt[e * 4 * LAT : (e + 1) * 4 * LAT, :], keys[mm]).reshape(4, LAT, CB)
                + bias[...][None]
                for mm, e in tags
            }
            peaks = {t: jnp.max(scores[t], axis=-1, keepdims=True) for t in tags}
            weights = {t: jnp.exp(scores[t] - peaks[t]).astype(BF16) for t in tags}
            for mm, e in tags:
                sums = jnp.dot(
                    weights[mm, e].reshape(4 * LAT, CB), both[mm, e], preferred_element_type=F32
                )
                for t in range(2):
                    a = sums[2 * t * LAT : (2 * t + 1) * LAT]
                    b = sums[(2 * t + 1) * LAT : (2 * t + 2) * LAT]
                    top = jnp.where(low, a[:, :CB], b[:, :CB])
                    bottom = jnp.where(low, a[:, CB:], b[:, CB:])
                    lanes = (e * 2 + t) * CB
                    att[pair * n + mm, :, lanes : lanes + CB] = (top / bottom).astype(BF16)
            return 0

        lax.fori_loop(0, STEP // n, some, 0)
        mixed = jnp.dot(
            att[...].reshape(STEP * LAT, D), w_out[...], preferred_element_type=F32
        ).reshape(STEP, LAT, D)
        latents = (q[...].astype(F32)[None] + mixed).reshape(STEP, CHAN, LG, D)
        for g in range(CHAN):
            lsend[g, c * STEP : (c + 1) * STEP] = latents[:, g].astype(BF16)
        for i, o in enumerate(OFFSETS):
            lat_copy(o, i, c).start()
        own_copy(c).start()

    for c in range(CHUNKS):
        for i in reversed(range(len(OFFSETS))):
            o = OFFSETS[i]
            kv_copy(o, i, c).wait_recv()
            spread(kv_recv, from_peer(o), c)
        attend(c, 2)
        if c >= 2:
            forward(c - 2)
    for c in range(CHUNKS - 2, CHUNKS):
        forward(c)

    def regrid(source, l):
        for f in range(FT):
            turn[l, f, 0 : SCAN * LG] = source[:, :, f * CB : (f + 1) * CB].reshape(SCAN * LG, CB)
        for i in range(LG):
            for f in range(FT):
                grid_f[0, l, i, f, 8 : 8 + WIDE] = turn[l, f, pl.ds(i, WIDE, stride=LG), :]

    for c in range(CHUNKS):
        for s in range(CHAN):
            if not (s // 2 < DEEP or s // 2 >= LINES - DEEP):
                await_latents(s, c)
    for l in range(LINES):
        regrid(lrecv[l].reshape(SCAN, LG, D).astype(F32), l + DEEP)

    def halo_copy(c, half, way):
        return pltpu.make_async_remote_copy(
            src_ref=hsend.at[c - DEEP, half, way],
            dst_ref=hrecv.at[c - DEEP, half, way],
            send_sem=h_ssem.at[c - DEEP, half, way],
            recv_sem=h_rsem.at[c - DEEP, half, way],
            device_id=(ways[way], me),
            device_id_type=MESH,
        )

    def out_copy(l):
        return pltpu.make_async_copy(outb.at[l], out_h.at[l], out_sem.at[l])

    def clear_pair(c, half, out):
        now, later = c % 2, (c + 1) % 2
        apart = CLEAR - 1 - 2 * out
        own = out - DEEP + 1
        final = c == LAYERS - 1

        def stencil(n):
            l = out + n * apart
            for f in range(FT):
                for t in range(WIDE // 8):
                    cs = [coef[c, l, f, k, 8 * t : 8 * t + 8] for k in range(9)]
                    for i in range(HALF):
                        total = None
                        for k in range(9):
                            term = cs[k] * grid_f[
                                now, l + k // 3, half * HALF + i, f, pl.ds(7 + 8 * t + k % 3, 8), :
                            ]
                            total = term if total is None else total + term
                        st[n, i, 8 * t : 8 * t + 8, f * CB : (f + 1) * CB] = total.astype(BF16)

        def finish(n, update):
            l = out + n * apart
            for i in range(HALF):
                for f in range(FT):
                    lanes = slice(f * CB, (f + 1) * CB)
                    centre = grid_f[now, l + 1, half * HALF + i, f, 8 : 8 + WIDE]
                    cleared = (centre + update[i, :, lanes]).astype(BF16)
                    wide = cleared.astype(F32)
                    if final:
                        at = pl.ds(pl.multiple_of((half * HALF + i) * WIDE, WIDE), WIDE)
                        last[l - DEEP + 1, f, at] = wide
                    else:
                        if own < 0:
                            wide = jnp.where(comes[1 - n], wide, 0.0)
                        grid_f[later, l + 1, half * HALF + i, f, 8 : 8 + WIDE] = wide
                        if own == 0 and c + 1 >= DEEP:
                            hsend[c + 1 - DEEP, half, n, i, :, lanes] = cleared

        def mix(n):
            return jnp.dot(
                st[n].reshape(HALF * WIDE, D), w_mix[c], preferred_element_type=F32
            ).reshape(HALF, WIDE, D)

        stencil(0)
        first = mix(0)
        stencil(1)
        finish(0, first)
        finish(1, mix(1))
        if own == 0 and not final and c + 1 >= DEEP:
            for way in range(2):

                @pl.when(sends[way])
                def _():
                    halo_copy(c + 1, half, way).start()

    def finish_pair(first, apart):
        def column(p, _):
            for n in range(2):
                for f in range(FT):
                    rows = last[first + n * apart, f, pl.ds(p, LG, stride=WIDE), :]
                    outb[first + n * apart, p, :, f * CB : (f + 1) * CB] = rows.astype(BF16)
            return 0

        lax.fori_loop(0, SCAN, column, 0)
        for n in range(2):
            out_copy(first + n * apart).start()

    def take_near():
        for way in range(2):
            base = (DEEP + LINES, 0)[way]

            @pl.when(comes[way])
            def _():
                for n in range(CHUNKS):
                    near_copy(n, way).wait_recv()
                for d in range(DEEP):
                    regrid(near[way, d].reshape(SCAN, LG, D).astype(F32), base + d)

            @pl.when(jnp.logical_not(comes[way]))
            def _():
                for d in range(DEEP):
                    for i in range(LG):
                        grid_f[0, base + d, i, :, 8 : 8 + WIDE] = jnp.zeros((FT, WIDE, CB), F32)

    def take_halo(c, half, way):
        edge = (DEEP + LINES, DEEP - 1)[way]
        own = pl.ds(half * HALF, HALF)

        @pl.when(comes[way])
        def _():
            halo_copy(c, half, way).wait_recv()
            for f in range(FT):
                grid_f[c % 2, edge, own, f, 8 : 8 + WIDE] = hrecv[
                    c - DEEP, half, way, :, :, f * CB : (f + 1) * CB
                ].astype(F32)

        @pl.when(jnp.logical_not(comes[way]))
        def _():
            for f in range(FT):
                grid_f[c % 2, edge, own, f, 8 : 8 + WIDE] = jnp.zeros((HALF, WIDE, CB), F32)

    inner, outer = DEEP, DEEP - 1

    def clear_both(c, out):
        def one(half, _):
            clear_pair(c, half, out)
            return 0

        lax.fori_loop(0, 2, one, 0)

    def clear_with_halo(c):
        def one(half, _):
            for way in range(2):
                take_halo(c, half, way)
            clear_pair(c, half, outer)
            return 0

        lax.fori_loop(0, 2, one, 0)

    clear_both(0, inner)
    take_near()
    for out in range(outer, -1, -1):
        clear_both(0, out)
    for c in range(1, LAYERS):
        if c < DEEP:
            for out in range(c, DEEP + 1):
                clear_both(c, out)
                if out == inner and c == LAYERS - 1:
                    finish_pair(1, 1)
        else:
            clear_both(c, inner)
            if c == LAYERS - 1:
                finish_pair(1, 1)
            clear_with_halo(c)
    finish_pair(0, LINES - 1)

    for i, o in enumerate(OFFSETS):
        for c in range(CHUNKS):
            kv_copy(o, i, c).wait_send()
            lat_copy(o, i, c).wait_send()
    for way in range(2):

        @pl.when(sends[way])
        def _():
            vm_copy(way).wait_send()
            for c in range(CHUNKS):
                near_copy(c, way).wait_send()
            for c in range(DEEP, LAYERS):
                for half in range(2):
                    halo_copy(c, half, way).wait_send()

    for l in range(LINES):
        out_copy(l).wait()


def local(tracks, radiance, w_key, w_value, latent_query, band_blocks, band_count, valid_mask, w_out, conv_taps, w_mix):
    hbm = pl.BlockSpec(memory_space=pl.ANY)
    vmem = pltpu.VMEM
    dma = pltpu.SemaphoreType.DMA
    peers = len(OFFSETS)
    return pl.pallas_call(
        functools.partial(kernel, tracks),
        out_shape=jax.ShapeDtypeStruct((LINES, SCAN, LG, D), BF16),
        in_specs=[hbm] * 10,
        out_specs=hbm,
        scratch_shapes=[
            vmem((SCAN, BLK, LINES, CB), BF16),
            vmem((BLK, CB, CB), BF16),
            vmem((BLK, CB, CB), BF16),
            vmem((LAT, D), BF16),
            vmem((CHAN, MAXB), jnp.int32),
            pltpu.SMEM((CHAN,), jnp.int32),
            vmem((9, LINES, SCAN), jnp.int32),
            vmem((D, D), BF16),
            vmem((9, LAYERS, D), F32),
            vmem((LAYERS, D, D), BF16),
            vmem((2, 9, LINES, SCAN), jnp.int32),
            vmem((SCAN * BLK * LINES + 72, CB), F32),
            vmem((CHAN, CHUNKS, 2, BLK, STEP, CB), BF16),
            vmem((CHAN, CHUNKS, 2, BLK, STEP, CB), BF16),
            vmem((CHUNKS, CB * STEP, CB), F32),
            vmem((CHUNKS, CB * STEP, CB), F32),
            vmem((HEADS * LAT, CB), BF16),
            vmem((LAT, CB), F32),
            vmem((STEP, LAT, D), BF16),
            vmem((CHAN, ROWS, LG, D), BF16),
            vmem((LINES, 2, PER, LG, D), BF16),
            vmem((2, DEEP, 2, PER, LG, D), BF16),
            vmem((3, CB, CB), F32),
            vmem((CLEAR, 9, WIDE, CB), F32),
            vmem((LAYERS, CLEAR, FT, 9, WIDE, CB), F32),
            vmem((ALL, FT, WIDE * LG, CB), F32),
            vmem((2, ALL, LG, FT, WIDE + 16, CB), F32),
            vmem((2, HALF, WIDE, D), BF16),
            vmem((EXCH, 2, 2, HALF, WIDE, D), BF16),
            vmem((EXCH, 2, 2, HALF, WIDE, D), BF16),
            vmem((LINES, FT, LG * WIDE, CB), F32),
            vmem((LINES, SCAN, LG, D), BF16),
            dma((10,)),
            dma((CHUNKS, peers)), dma((CHUNKS, peers)),
            dma((CHUNKS, peers)), dma((CHUNKS, CHAN)),
            dma((CHUNKS, 2)), dma((CHUNKS, 2)),
            dma((2,)), dma((2,)),
            dma((EXCH, 2, 2)), dma((EXCH, 2, 2)),
            dma((LINES,)),
        ],
        compiler_params=pltpu.CompilerParams(
            collective_id=0, has_side_effects=True, vmem_limit_bytes=60 * 1024 * 1024
        ),
    )(
        jnp.transpose(radiance, (1, 2, 0, 3)), w_key, w_value, latent_query, band_blocks, band_count,
        jnp.transpose(valid_mask, (2, 0, 1)), w_out, jnp.transpose(conv_taps, (1, 0, 2)), w_mix,
    )


def solution(mesh):
    return jax.shard_map(
        functools.partial(local, mesh.shape["track"]),
        mesh=mesh,
        in_specs=(
            P("track", None, "chan", None),
            P("chan", None, None),
            P("chan", None, None),
            P(),
            P(),
            P(),
            P("track", None, None),
            P(),
            P(),
            P(),
        ),
        out_specs=P("track", None, "chan", None),
        check_vma=False,
    )
```

```python
import functools

import jax
import jax.numpy as jnp
from jax import lax
from jax.experimental import pallas as pl
from jax.experimental.pallas import tpu as pltpu
from jax.sharding import PartitionSpec as P

HEADS = 8
HEAD_DIM = 64
NBLK = 72
LAYERS = 3
DEEP = 2
NX, NY = 4, 2
CHAN = NX * NY
LINES, SCAN = 4, 30
WIDE = 32
PER = LINES * SCAN // CHAN
ROWS = 16
BLK = NBLK // CHAN
LAT, D, CB = 64, 512, 128
FT = D // CB
LG = LAT // CHAN
MAXB = 48
HALF = LG // 2
STEP = 4
CHUNKS = ROWS // STEP
EXCH = max(LAYERS - DEEP, 1)
ALL = LINES + 2 * DEEP
CLEAR = ALL - 2
COLUMNS = 10
MASKED = -1e30
MESH = pl.DeviceIdType.MESH
OFFSETS = ((2, 1), (2, 0), (1, 1), (3, 1), (1, 0), (3, 0), (0, 1))
BF16, F32 = jnp.bfloat16, jnp.float32


def nt_dot(a, b):
    return lax.dot_general(a, b, (((1,), (1,)), ((), ())), preferred_element_type=F32)


def chunk_at(c):
    return pl.ds(c * STEP, min(STEP, PER - c * STEP))


def kernel(
    tracks, rad_h, wk_h, wv_h, q_h, bb_h, cnt_h, vm_h, w_out_h, taps_h, w_mix_h, out_h,
    rad, wk, wv, q, bb, cnt, vm, w_out, taps, w_mix, vm_near,
    xf, kv_send, kv_recv, kf, vf, qbt, bias, att, lsend, lrecv, near,
    vmf, mb, coef, turn, grid_f, st, hsend, hrecv, last, outb,
    in_sem, kv_ssem, kv_rsem, l_ssem, l_rsem, n_ssem, n_rsem, v_ssem, v_rsem, h_ssem, h_rsem, out_sem,
):
    track, me = lax.axis_index("track"), lax.axis_index("chan")
    x, y = me // NY, me % NY
    up, down = (track + tracks - 1) % tracks, (track + 1) % tracks
    ways = (up, down)
    not_first, not_last = track > 0, track < tracks - 1
    sends, comes = (not_first, not_last), (not_last, not_first)

    def to_peer(o):
        return ((x + o[0]) % NX) * NY + (y + o[1]) % NY

    def from_peer(o):
        return ((x + NX - o[0]) % NX) * NY + (y + NY - o[1]) % NY

    barrier = pltpu.get_barrier_semaphore()
    for o in OFFSETS:
        pl.semaphore_signal(barrier, inc=1, device_id=(track, to_peer(o)), device_id_type=MESH)
    for way in range(2):

        @pl.when(sends[way])
        def _():
            pl.semaphore_signal(barrier, inc=1, device_id=(ways[way], me), device_id_type=MESH)

    loads = [
        pltpu.make_async_copy(src, dst, in_sem.at[i])
        for i, (src, dst) in enumerate(
            (
                (rad_h, rad), (wk_h, wk), (wv_h, wv), (q_h, q), (bb_h, bb), (cnt_h, cnt),
                (vm_h, vm), (taps_h, taps), (w_out_h, w_out), (w_mix_h, w_mix),
            )
        )
    ]
    for load in loads:
        load.start()

    xf[pl.ds(SCAN * BLK * LINES, 72), :] = jnp.zeros((72, CB), F32)
    loads[0].wait()
    xf[pl.ds(0, SCAN * BLK * LINES), :] = rad[...].astype(F32).reshape(SCAN * BLK * LINES, CB)
    loads[1].wait()
    loads[2].wait()

    for b in range(BLK):
        rows = jnp.concatenate(
            [
                xf[pl.ds((j % 2) * PER * BLK * LINES + b * LINES + j // 2, ROWS, stride=BLK * LINES), :]
                for j in range(CHAN)
            ],
            axis=0,
        )
        inverse = lax.rsqrt(jnp.mean(rows * rows, axis=-1, keepdims=True) + 1e-05)
        normed = (rows * inverse).astype(BF16)
        keys = jnp.dot(rows.astype(BF16), wk[b], preferred_element_type=F32)
        values = jnp.dot(normed, wv[b], preferred_element_type=F32)
        kv_send[:, :, 0, b] = keys.astype(BF16).reshape(CHAN, CHUNKS, STEP, CB)
        kv_send[:, :, 1, b] = values.astype(BF16).reshape(CHAN, CHUNKS, STEP, CB)

    pl.semaphore_wait(barrier, len(OFFSETS) + not_first.astype(jnp.int32) + not_last.astype(jnp.int32))

    def kv_copy(o, i, c):
        return pltpu.make_async_remote_copy(
            src_ref=kv_send.at[to_peer(o), c],
            dst_ref=kv_recv.at[me, c],
            send_sem=kv_ssem.at[c, i],
            recv_sem=kv_rsem.at[c, i],
            device_id=(track, to_peer(o)),
            device_id_type=MESH,
        )

    for c in range(CHUNKS):
        for i, o in enumerate(OFFSETS):
            kv_copy(o, i, c).start()

    for load in loads[3:]:
        load.wait()

    def vm_copy(way):
        return pltpu.make_async_remote_copy(
            src_ref=vm,
            dst_ref=vm_near.at[way],
            send_sem=v_ssem.at[way],
            recv_sem=v_rsem.at[way],
            device_id=(ways[way], me),
            device_id_type=MESH,
        )

    for way in range(2):

        @pl.when(sends[way])
        def _():
            vm_copy(way).start()

    lane = lax.broadcasted_iota(jnp.int32, (LAT, CB), 1)
    low = lane < HEAD_DIM
    for h in range(HEADS):
        e = h // 4
        part = q[:, (h // 2) * CB : (h // 2 + 1) * CB].astype(F32) * HEAD_DIM**-0.5
        if h % 2 != e:
            part = pltpu.roll(part, HEAD_DIM, 1)
        part = jnp.where(low if e == 0 else jnp.logical_not(low), part, 0.0)
        qbt[h * LAT : (h + 1) * LAT, :] = part.astype(BF16)

    group = lax.broadcasted_iota(jnp.int32, (CHAN, MAXB), 0)
    slot = lax.broadcasted_iota(jnp.int32, (CHAN, MAXB), 1)
    used = jnp.zeros((CHAN, MAXB), jnp.int32)
    for g in range(CHAN):
        used = jnp.where(group == g, cnt[g], used)
    blocks = jnp.where(slot < used, bb[...], -1)
    block_of = lax.broadcasted_iota(jnp.int32, (CHAN, CB), 1)
    allowed = jnp.full((CHAN, CB), MASKED, F32)
    for j in range(MAXB):
        allowed = jnp.where(blocks[:, j : j + 1] == block_of, 0.0, allowed)
    for g in range(CHAN):
        bias[g * LG : (g + 1) * LG, :] = jnp.broadcast_to(allowed[g : g + 1], (LG, CB))

    kf[:, pl.ds(NBLK * STEP, (CB - NBLK) * STEP), :] = jnp.zeros((CHUNKS, (CB - NBLK) * STEP, CB), F32)
    vf[:, pl.ds(NBLK * STEP, (CB - NBLK) * STEP), :] = jnp.zeros((CHUNKS, (CB - NBLK) * STEP, CB), F32)

    def spread(ref, s, c):
        at = pl.ds(s * (BLK * STEP), BLK * STEP)
        kf[c, at, :] = ref[s, c, 0].astype(F32).reshape(BLK * STEP, CB)
        vf[c, at, :] = ref[s, c, 1].astype(F32).reshape(BLK * STEP, CB)

    for c in range(CHUNKS):
        spread(kv_send, me, c)

    def validity(slot, source, lines):
        vmf[slot] = jnp.zeros((CB, CB), F32)
        for k in range(9):
            vmf[slot, k * LINES : (k + 1) * LINES, 0:SCAN] = source(k).astype(F32)
        turned = vmf[slot].T
        for l, to in lines:
            for k in range(9):
                col = turned[:WIDE, k * LINES + l : k * LINES + l + 1]
                mb[to, k] = jnp.broadcast_to(col, (WIDE, CB))

    validity(0, lambda k: vm[k], [(l, l + DEEP - 1) for l in range(LINES)])
    for way in range(2):

        @pl.when(comes[way])
        def _():
            vm_copy(way).wait_recv()

            if way == 0:
                lines = [(l, DEEP - 1 + LINES + l) for l in range(DEEP - 1)]
            else:
                lines = [(LINES - DEEP + 1 + l, l) for l in range(DEEP - 1)]
            validity(1 + way, lambda k: vm_near[way, k], lines)

        @pl.when(jnp.logical_not(comes[way]))
        def _():
            for l in range(DEEP - 1):
                mb[l if way == 1 else DEEP - 1 + LINES + l] = jnp.zeros((9, WIDE, CB), F32)

    def coefficients(l, _):
        for c in range(LAYERS):
            for f in range(FT):
                for k in range(9):
                    coef[c, l, f, k] = mb[l, k] * taps[k, c : c + 1, f * CB : (f + 1) * CB]
        return 0

    lax.fori_loop(0, CLEAR, coefficients, 0)

    def borders(l, _):
        for s in range(2):
            for i in range(LG):
                grid_f[s, l, i, :, 0:8] = jnp.zeros((FT, 8, CB), F32)
                grid_f[s, l, i, :, 8 + WIDE : 16 + WIDE] = jnp.zeros((FT, 8, CB), F32)
        turn[l, :, SCAN * LG : WIDE * LG] = jnp.zeros((FT, (WIDE - SCAN) * LG, CB), F32)
        return 0

    lax.fori_loop(0, ALL, borders, 0)

    line_me, side_me = me // 2, me % 2

    def lat_copy(o, i, c):
        return pltpu.make_async_remote_copy(
            src_ref=lsend.at[to_peer(o), chunk_at(c)],
            dst_ref=lrecv.at[line_me, side_me, chunk_at(c)],
            send_sem=l_ssem.at[c, i],
            recv_sem=l_rsem.at[c, me],
            device_id=(track, to_peer(o)),
            device_id_type=MESH,
        )

    def own_copy(c):
        return pltpu.make_async_copy(
            lsend.at[me, chunk_at(c)],
            lrecv.at[line_me, side_me, chunk_at(c)],
            l_rsem.at[c, me],
        )

    def await_latents(s, c):
        pltpu.make_async_copy(
            lsend.at[s, chunk_at(c)], lrecv.at[s // 2, s % 2, chunk_at(c)], l_rsem.at[c, s]
        ).wait()

    def near_copy(c, way):
        return pltpu.make_async_remote_copy(
            src_ref=lrecv.at[pl.ds(way * (LINES - DEEP), DEEP), :, chunk_at(c)],
            dst_ref=near.at[way, :, :, chunk_at(c)],
            send_sem=n_ssem.at[c, way],
            recv_sem=n_rsem.at[c, way],
            device_id=(ways[way], me),
            device_id_type=MESH,
        )

    def forward(c):
        for s in range(CHAN):
            if s // 2 < DEEP or s // 2 >= LINES - DEEP:
                await_latents(s, c)
        for way in range(2):

            @pl.when(sends[way])
            def _():
                near_copy(c, way).start()

    ones = jnp.ones((CB, CB), BF16)
    low_v = lax.broadcasted_iota(jnp.int32, (CB, CB), 1) < HEAD_DIM

    def attend(c, n):
        def some(pair, _):
            tags = [(mm, e) for mm in range(n) for e in range(2)]
            at = [pair * n + mm for mm in range(n)]
            keys = [kf[c, pl.ds(a, CB, stride=STEP), :].astype(BF16) for a in at]
            values = [vf[c, pl.ds(a, CB, stride=STEP), :] for a in at]
            swapped = [pltpu.roll(v, HEAD_DIM, 1) for v in values]
            both = {
                (mm, e): jnp.concatenate(
                    [
                        (
                            jnp.where(low_v, values[mm], swapped[mm])
                            if e == 0
                            else jnp.where(low_v, swapped[mm], values[mm])
                        ).astype(BF16),
                        ones,
                    ],
                    axis=1,
                )
                for mm, e in tags
            }
            scores = {
                (mm, e): nt_dot(qbt[e * 4 * LAT : (e + 1) * 4 * LAT, :], keys[mm]).reshape(4, LAT, CB)
                + bias[...][None]
                for mm, e in tags
            }
            peaks = {t: jnp.max(scores[t], axis=-1, keepdims=True) for t in tags}
            weights = {t: jnp.exp(scores[t] - peaks[t]).astype(BF16) for t in tags}
            for mm, e in tags:
                sums = jnp.dot(
                    weights[mm, e].reshape(4 * LAT, CB), both[mm, e], preferred_element_type=F32
                )
                for t in range(2):
                    a = sums[2 * t * LAT : (2 * t + 1) * LAT]
                    b = sums[(2 * t + 1) * LAT : (2 * t + 2) * LAT]
                    top = jnp.where(low, a[:, :CB], b[:, :CB])
                    bottom = jnp.where(low, a[:, CB:], b[:, CB:])
                    lanes = (e * 2 + t) * CB
                    att[pair * n + mm, :, lanes : lanes + CB] = (top / bottom).astype(BF16)
            return 0

        lax.fori_loop(0, STEP // n, some, 0)
        mixed = jnp.dot(
            att[...].reshape(STEP * LAT, D), w_out[...], preferred_element_type=F32
        ).reshape(STEP, LAT, D)
        latents = (q[...].astype(F32)[None] + mixed).reshape(STEP, CHAN, LG, D)
        for g in range(CHAN):
            lsend[g, c * STEP : (c + 1) * STEP] = latents[:, g].astype(BF16)
        for i, o in enumerate(OFFSETS):
            lat_copy(o, i, c).start()
        own_copy(c).start()

    for c in range(CHUNKS):
        for i in reversed(range(len(OFFSETS))):
            o = OFFSETS[i]
            kv_copy(o, i, c).wait_recv()
            spread(kv_recv, from_peer(o), c)
        attend(c, 2)
        if c >= 2:
            forward(c - 2)
    for c in range(CHUNKS - 2, CHUNKS):
        forward(c)

    def regrid(source, l):
        for f in range(FT):
            turn[l, f, 0 : SCAN * LG] = source[:, :, f * CB : (f + 1) * CB].reshape(SCAN * LG, CB)
        for i in range(LG):
            for f in range(FT):
                grid_f[0, l, i, f, 8 : 8 + WIDE] = turn[l, f, pl.ds(i, WIDE, stride=LG), :]

    for c in range(CHUNKS):
        for s in range(CHAN):
            if not (s // 2 < DEEP or s // 2 >= LINES - DEEP):
                await_latents(s, c)
    for l in range(LINES):
        regrid(lrecv[l].reshape(SCAN, LG, D).astype(F32), l + DEEP)

    def halo_copy(c, half, way):
        return pltpu.make_async_remote_copy(
            src_ref=hsend.at[c - DEEP, half, way],
            dst_ref=hrecv.at[c - DEEP, half, way],
            send_sem=h_ssem.at[c - DEEP, half, way],
            recv_sem=h_rsem.at[c - DEEP, half, way],
            device_id=(ways[way], me),
            device_id_type=MESH,
        )

    def out_copy(l):
        return pltpu.make_async_copy(outb.at[l], out_h.at[l], out_sem.at[l])

    def clear_pair(c, half, out):
        now, later = c % 2, (c + 1) % 2
        apart = CLEAR - 1 - 2 * out
        own = out - DEEP + 1
        final = c == LAYERS - 1

        def stencil(n):
            l = out + n * apart
            for f in range(FT):
                for t in range(WIDE // 8):
                    cs = [coef[c, l, f, k, 8 * t : 8 * t + 8] for k in range(9)]
                    for i in range(HALF):
                        total = None
                        for k in range(9):
                            term = cs[k] * grid_f[
                                now, l + k // 3, half * HALF + i, f, pl.ds(7 + 8 * t + k % 3, 8), :
                            ]
                            total = term if total is None else total + term
                        st[n, i, 8 * t : 8 * t + 8, f * CB : (f + 1) * CB] = total.astype(BF16)

        def finish(n, update):
            l = out + n * apart
            for i in range(HALF):
                for f in range(FT):
                    lanes = slice(f * CB, (f + 1) * CB)
                    centre = grid_f[now, l + 1, half * HALF + i, f, 8 : 8 + WIDE]
                    cleared = (centre + update[i, :, lanes]).astype(BF16)
                    wide = cleared.astype(F32)
                    if final:
                        at = pl.ds(pl.multiple_of((half * HALF + i) * WIDE, WIDE), WIDE)
                        last[l - DEEP + 1, f, at] = wide
                    else:
                        if own < 0:
                            wide = jnp.where(comes[1 - n], wide, 0.0)
                        grid_f[later, l + 1, half * HALF + i, f, 8 : 8 + WIDE] = wide
                        if own == 0 and c + 1 >= DEEP:
                            hsend[c + 1 - DEEP, half, n, i, :, lanes] = cleared

        def mix(n):
            return jnp.dot(
                st[n].reshape(HALF * WIDE, D), w_mix[c], preferred_element_type=F32
            ).reshape(HALF, WIDE, D)

        stencil(0)
        first = mix(0)
        stencil(1)
        finish(0, first)
        finish(1, mix(1))
        if own == 0 and not final and c + 1 >= DEEP:
            for way in range(2):

                @pl.when(sends[way])
                def _():
                    halo_copy(c + 1, half, way).start()

    def finish_pair(first, apart):
        def columns(group, _):
            for d in range(COLUMNS):
                p = group * COLUMNS + d
                for n in range(2):
                    for f in range(FT):
                        rows = last[first + n * apart, f, pl.ds(p, LG, stride=WIDE), :]
                        outb[first + n * apart, p, :, f * CB : (f + 1) * CB] = rows.astype(BF16)
            return 0

        lax.fori_loop(0, SCAN // COLUMNS, columns, 0)
        for n in range(2):
            out_copy(first + n * apart).start()

    def take_near():
        for way in range(2):
            base = (DEEP + LINES, 0)[way]

            @pl.when(comes[way])
            def _():
                for n in range(CHUNKS):
                    near_copy(n, way).wait_recv()
                for d in range(DEEP):
                    regrid(near[way, d].reshape(SCAN, LG, D).astype(F32), base + d)

            @pl.when(jnp.logical_not(comes[way]))
            def _():
                for d in range(DEEP):
                    for i in range(LG):
                        grid_f[0, base + d, i, :, 8 : 8 + WIDE] = jnp.zeros((FT, WIDE, CB), F32)

    def take_halo(c, half, way):
        edge = (DEEP + LINES, DEEP - 1)[way]
        own = pl.ds(half * HALF, HALF)

        @pl.when(comes[way])
        def _():
            halo_copy(c, half, way).wait_recv()
            for f in range(FT):
                grid_f[c % 2, edge, own, f, 8 : 8 + WIDE] = hrecv[
                    c - DEEP, half, way, :, :, f * CB : (f + 1) * CB
                ].astype(F32)

        @pl.when(jnp.logical_not(comes[way]))
        def _():
            for f in range(FT):
                grid_f[c % 2, edge, own, f, 8 : 8 + WIDE] = jnp.zeros((HALF, WIDE, CB), F32)

    inner, outer = DEEP, DEEP - 1

    def clear_both(c, out):
        def one(half, _):
            clear_pair(c, half, out)
            return 0

        lax.fori_loop(0, 2, one, 0)

    def clear_with_halo(c):
        def one(half, _):
            for way in range(2):
                take_halo(c, half, way)
            clear_pair(c, half, outer)
            return 0

        lax.fori_loop(0, 2, one, 0)

    clear_both(0, inner)
    take_near()

    def up_to_halo(half, _):
        for c in range(DEEP):
            for out in range(outer, c - 1, -1):
                clear_pair(c, half, out)
        return 0

    lax.fori_loop(0, 2, up_to_halo, 0)
    clear_both(1, inner)
    clear_both(2, inner)
    finish_pair(1, 1)
    clear_with_halo(2)
    finish_pair(0, LINES - 1)

    for i, o in enumerate(OFFSETS):
        for c in range(CHUNKS):
            kv_copy(o, i, c).wait_send()
            lat_copy(o, i, c).wait_send()
    for way in range(2):

        @pl.when(sends[way])
        def _():
            vm_copy(way).wait_send()
            for c in range(CHUNKS):
                near_copy(c, way).wait_send()
            for c in range(DEEP, LAYERS):
                for half in range(2):
                    halo_copy(c, half, way).wait_send()

    for l in range(LINES):
        out_copy(l).wait()


def local(tracks, radiance, w_key, w_value, latent_query, band_blocks, band_count, valid_mask, w_out, conv_taps, w_mix):
    hbm = pl.BlockSpec(memory_space=pl.ANY)
    vmem = pltpu.VMEM
    dma = pltpu.SemaphoreType.DMA
    peers = len(OFFSETS)
    return pl.pallas_call(
        functools.partial(kernel, tracks),
        out_shape=jax.ShapeDtypeStruct((LINES, SCAN, LG, D), BF16),
        in_specs=[hbm] * 10,
        out_specs=hbm,
        scratch_shapes=[
            vmem((SCAN, BLK, LINES, CB), BF16),
            vmem((BLK, CB, CB), BF16),
            vmem((BLK, CB, CB), BF16),
            vmem((LAT, D), BF16),
            vmem((CHAN, MAXB), jnp.int32),
            pltpu.SMEM((CHAN,), jnp.int32),
            vmem((9, LINES, SCAN), jnp.int32),
            vmem((D, D), BF16),
            vmem((9, LAYERS, D), F32),
            vmem((LAYERS, D, D), BF16),
            vmem((2, 9, LINES, SCAN), jnp.int32),
            vmem((SCAN * BLK * LINES + 72, CB), F32),
            vmem((CHAN, CHUNKS, 2, BLK, STEP, CB), BF16),
            vmem((CHAN, CHUNKS, 2, BLK, STEP, CB), BF16),
            vmem((CHUNKS, CB * STEP, CB), F32),
            vmem((CHUNKS, CB * STEP, CB), F32),
            vmem((HEADS * LAT, CB), BF16),
            vmem((LAT, CB), F32),
            vmem((STEP, LAT, D), BF16),
            vmem((CHAN, ROWS, LG, D), BF16),
            vmem((LINES, 2, PER, LG, D), BF16),
            vmem((2, DEEP, 2, PER, LG, D), BF16),
            vmem((3, CB, CB), F32),
            vmem((CLEAR, 9, WIDE, CB), F32),
            vmem((LAYERS, CLEAR, FT, 9, WIDE, CB), F32),
            vmem((ALL, FT, WIDE * LG, CB), F32),
            vmem((2, ALL, LG, FT, WIDE + 16, CB), F32),
            vmem((2, HALF, WIDE, D), BF16),
            vmem((EXCH, 2, 2, HALF, WIDE, D), BF16),
            vmem((EXCH, 2, 2, HALF, WIDE, D), BF16),
            vmem((LINES, FT, LG * WIDE, CB), F32),
            vmem((LINES, SCAN, LG, D), BF16),
            dma((10,)),
            dma((CHUNKS, peers)), dma((CHUNKS, peers)),
            dma((CHUNKS, peers)), dma((CHUNKS, CHAN)),
            dma((CHUNKS, 2)), dma((CHUNKS, 2)),
            dma((2,)), dma((2,)),
            dma((EXCH, 2, 2)), dma((EXCH, 2, 2)),
            dma((LINES,)),
        ],
        compiler_params=pltpu.CompilerParams(
            collective_id=0, has_side_effects=True, vmem_limit_bytes=60 * 1024 * 1024
        ),
    )(
        jnp.transpose(radiance, (1, 2, 0, 3)), w_key, w_value, latent_query, band_blocks, band_count,
        jnp.transpose(valid_mask, (2, 0, 1)), w_out, jnp.transpose(conv_taps, (1, 0, 2)), w_mix,
    )


def solution(mesh):
    return jax.shard_map(
        functools.partial(local, mesh.shape["track"]),
        mesh=mesh,
        in_specs=(
            P("track", None, "chan", None),
            P("chan", None, None),
            P("chan", None, None),
            P(),
            P(),
            P(),
            P("track", None, None),
            P(),
            P(),
            P(),
        ),
        out_specs=P("track", None, "chan", None),
        check_vma=False,
    )
```

```python
import functools

import jax
import jax.numpy as jnp
from jax import lax
from jax.experimental import pallas as pl
from jax.experimental.pallas import tpu as pltpu
from jax.sharding import PartitionSpec as P

HEADS = 8
HEAD_DIM = 64
NBLK = 72
LAYERS = 3
DEEP = 2
NX, NY = 4, 2
CHAN = NX * NY
LINES, SCAN = 4, 30
WIDE = 32
PER = LINES * SCAN // CHAN
ROWS = 16
BLK = NBLK // CHAN
LAT, D, CB = 64, 512, 128
FT = D // CB
LG = LAT // CHAN
MAXB = 48
HALF = LG // 2
STEP = 4
CHUNKS = ROWS // STEP
EXCH = max(LAYERS - DEEP, 1)
ALL = LINES + 2 * DEEP
CLEAR = ALL - 2
COLUMNS = 10
MASKED = -1e30
MESH = pl.DeviceIdType.MESH
OFFSETS = ((2, 1), (2, 0), (1, 1), (3, 1), (1, 0), (3, 0), (0, 1))
BF16, F32 = jnp.bfloat16, jnp.float32


def nt_dot(a, b):
    return lax.dot_general(a, b, (((1,), (1,)), ((), ())), preferred_element_type=F32)


def chunk_at(c):
    return pl.ds(c * STEP, min(STEP, PER - c * STEP))


def kernel(
    tracks, rad_h, wk_h, wv_h, q_h, bb_h, cnt_h, vm_h, w_out_h, taps_h, w_mix_h, out_h,
    rad, wk, wv, q, bb, cnt, vm, w_out, taps, w_mix, vm_near,
    xf, kv_send, kv_recv, kf, vf, qbt, bias, att, lsend, lrecv, near,
    vmf, mb, coef, turn, grid_f, st, hsend, hrecv, last, outb,
    in_sem, kv_ssem, kv_rsem, l_ssem, l_rsem, n_ssem, n_rsem, v_ssem, v_rsem, h_ssem, h_rsem, out_sem,
):
    track, me = lax.axis_index("track"), lax.axis_index("chan")
    x, y = me // NY, me % NY
    up, down = (track + tracks - 1) % tracks, (track + 1) % tracks
    ways = (up, down)
    not_first, not_last = track > 0, track < tracks - 1
    sends, comes = (not_first, not_last), (not_last, not_first)

    def to_peer(o):
        return ((x + o[0]) % NX) * NY + (y + o[1]) % NY

    def from_peer(o):
        return ((x + NX - o[0]) % NX) * NY + (y + NY - o[1]) % NY

    barrier = pltpu.get_barrier_semaphore()
    for o in OFFSETS:
        pl.semaphore_signal(barrier, inc=1, device_id=(track, to_peer(o)), device_id_type=MESH)
    for way in range(2):

        @pl.when(sends[way])
        def _():
            pl.semaphore_signal(barrier, inc=1, device_id=(ways[way], me), device_id_type=MESH)

    loads = [
        pltpu.make_async_copy(src, dst, in_sem.at[i])
        for i, (src, dst) in enumerate(
            (
                (rad_h, rad), (wk_h, wk), (wv_h, wv), (q_h, q), (bb_h, bb), (cnt_h, cnt),
                (vm_h, vm), (taps_h, taps), (w_out_h, w_out), (w_mix_h, w_mix),
            )
        )
    ]
    for load in loads[:8]:
        load.start()

    xf[pl.ds(SCAN * BLK * LINES, 72), :] = jnp.zeros((72, CB), F32)
    loads[0].wait()
    xf[pl.ds(0, SCAN * BLK * LINES), :] = rad[...].astype(F32).reshape(SCAN * BLK * LINES, CB)
    loads[1].wait()
    loads[2].wait()
    for load in loads[8:]:
        load.start()

    for b in range(BLK):
        rows = jnp.concatenate(
            [
                xf[pl.ds((j % 2) * PER * BLK * LINES + b * LINES + j // 2, ROWS, stride=BLK * LINES), :]
                for j in range(CHAN)
            ],
            axis=0,
        )
        inverse = lax.rsqrt(jnp.mean(rows * rows, axis=-1, keepdims=True) + 1e-05)
        normed = (rows * inverse).astype(BF16)
        keys = jnp.dot(rows.astype(BF16), wk[b], preferred_element_type=F32)
        values = jnp.dot(normed, wv[b], preferred_element_type=F32)
        kv_send[:, :, 0, b] = keys.astype(BF16).reshape(CHAN, CHUNKS, STEP, CB)
        kv_send[:, :, 1, b] = values.astype(BF16).reshape(CHAN, CHUNKS, STEP, CB)

    pl.semaphore_wait(barrier, len(OFFSETS) + not_first.astype(jnp.int32) + not_last.astype(jnp.int32))

    def kv_copy(o, i, c):
        return pltpu.make_async_remote_copy(
            src_ref=kv_send.at[to_peer(o), c],
            dst_ref=kv_recv.at[me, c],
            send_sem=kv_ssem.at[c, i],
            recv_sem=kv_rsem.at[c, i],
            device_id=(track, to_peer(o)),
            device_id_type=MESH,
        )

    for c in range(CHUNKS):
        for i, o in enumerate(OFFSETS):
            kv_copy(o, i, c).start()

    for load in loads[3:8]:
        load.wait()

    def vm_copy(way):
        return pltpu.make_async_remote_copy(
            src_ref=vm,
            dst_ref=vm_near.at[way],
            send_sem=v_ssem.at[way],
            recv_sem=v_rsem.at[way],
            device_id=(ways[way], me),
            device_id_type=MESH,
        )

    for way in range(2):

        @pl.when(sends[way])
        def _():
            vm_copy(way).start()

    lane = lax.broadcasted_iota(jnp.int32, (LAT, CB), 1)
    low = lane < HEAD_DIM
    for h in range(HEADS):
        e = h // 4
        part = q[:, (h // 2) * CB : (h // 2 + 1) * CB].astype(F32) * HEAD_DIM**-0.5
        if h % 2 != e:
            part = pltpu.roll(part, HEAD_DIM, 1)
        part = jnp.where(low if e == 0 else jnp.logical_not(low), part, 0.0)
        qbt[h * LAT : (h + 1) * LAT, :] = part.astype(BF16)

    group = lax.broadcasted_iota(jnp.int32, (CHAN, MAXB), 0)
    slot = lax.broadcasted_iota(jnp.int32, (CHAN, MAXB), 1)
    used = jnp.zeros((CHAN, MAXB), jnp.int32)
    for g in range(CHAN):
        used = jnp.where(group == g, cnt[g], used)
    blocks = jnp.where(slot < used, bb[...], -1)
    block_of = lax.broadcasted_iota(jnp.int32, (CHAN, CB), 1)
    allowed = jnp.full((CHAN, CB), MASKED, F32)
    for j in range(MAXB):
        allowed = jnp.where(blocks[:, j : j + 1] == block_of, 0.0, allowed)
    for g in range(CHAN):
        bias[g * LG : (g + 1) * LG, :] = jnp.broadcast_to(allowed[g : g + 1], (LG, CB))

    kf[:, pl.ds(NBLK * STEP, (CB - NBLK) * STEP), :] = jnp.zeros((CHUNKS, (CB - NBLK) * STEP, CB), F32)
    vf[:, pl.ds(NBLK * STEP, (CB - NBLK) * STEP), :] = jnp.zeros((CHUNKS, (CB - NBLK) * STEP, CB), F32)

    def spread(ref, s, c):
        at = pl.ds(s * (BLK * STEP), BLK * STEP)
        kf[c, at, :] = ref[s, c, 0].astype(F32).reshape(BLK * STEP, CB)
        vf[c, at, :] = ref[s, c, 1].astype(F32).reshape(BLK * STEP, CB)

    for c in range(CHUNKS):
        spread(kv_send, me, c)

    def validity(slot, source, lines):
        vmf[slot] = jnp.zeros((CB, CB), F32)
        for k in range(9):
            vmf[slot, k * LINES : (k + 1) * LINES, 0:SCAN] = source(k).astype(F32)
        turned = vmf[slot].T
        for l, to in lines:
            for k in range(9):
                col = turned[:WIDE, k * LINES + l : k * LINES + l + 1]
                mb[to, k] = jnp.broadcast_to(col, (WIDE, CB))

    validity(0, lambda k: vm[k], [(l, l + DEEP - 1) for l in range(LINES)])
    for way in range(2):

        @pl.when(comes[way])
        def _():
            vm_copy(way).wait_recv()

            if way == 0:
                lines = [(l, DEEP - 1 + LINES + l) for l in range(DEEP - 1)]
            else:
                lines = [(LINES - DEEP + 1 + l, l) for l in range(DEEP - 1)]
            validity(1 + way, lambda k: vm_near[way, k], lines)

        @pl.when(jnp.logical_not(comes[way]))
        def _():
            for l in range(DEEP - 1):
                mb[l if way == 1 else DEEP - 1 + LINES + l] = jnp.zeros((9, WIDE, CB), F32)

    def coefficients(l, _):
        for c in range(LAYERS):
            for f in range(FT):
                for k in range(9):
                    coef[c, l, f, k] = mb[l, k] * taps[k, c : c + 1, f * CB : (f + 1) * CB]
        return 0

    lax.fori_loop(0, CLEAR, coefficients, 0)

    def borders(l, _):
        for s in range(2):
            for i in range(LG):
                grid_f[s, l, i, :, 0:8] = jnp.zeros((FT, 8, CB), F32)
                grid_f[s, l, i, :, 8 + WIDE : 16 + WIDE] = jnp.zeros((FT, 8, CB), F32)
        turn[l, :, SCAN * LG : WIDE * LG] = jnp.zeros((FT, (WIDE - SCAN) * LG, CB), F32)
        return 0

    lax.fori_loop(0, ALL, borders, 0)

    line_me, side_me = me // 2, me % 2

    def lat_copy(o, i, c):
        return pltpu.make_async_remote_copy(
            src_ref=lsend.at[to_peer(o), chunk_at(c)],
            dst_ref=lrecv.at[line_me, side_me, chunk_at(c)],
            send_sem=l_ssem.at[c, i],
            recv_sem=l_rsem.at[c, me],
            device_id=(track, to_peer(o)),
            device_id_type=MESH,
        )

    def own_copy(c):
        return pltpu.make_async_copy(
            lsend.at[me, chunk_at(c)],
            lrecv.at[line_me, side_me, chunk_at(c)],
            l_rsem.at[c, me],
        )

    def await_latents(s, c):
        pltpu.make_async_copy(
            lsend.at[s, chunk_at(c)], lrecv.at[s // 2, s % 2, chunk_at(c)], l_rsem.at[c, s]
        ).wait()

    def near_copy(c, way):
        return pltpu.make_async_remote_copy(
            src_ref=lrecv.at[pl.ds(way * (LINES - DEEP), DEEP), :, chunk_at(c)],
            dst_ref=near.at[way, :, :, chunk_at(c)],
            send_sem=n_ssem.at[c, way],
            recv_sem=n_rsem.at[c, way],
            device_id=(ways[way], me),
            device_id_type=MESH,
        )

    def forward(c):
        for s in range(CHAN):
            if s // 2 < DEEP or s // 2 >= LINES - DEEP:
                await_latents(s, c)
        for way in range(2):

            @pl.when(sends[way])
            def _():
                near_copy(c, way).start()

    ones = jnp.ones((CB, CB), BF16)
    low_v = lax.broadcasted_iota(jnp.int32, (CB, CB), 1) < HEAD_DIM

    def attend(c, n):
        def some(pair, _):
            tags = [(mm, e) for mm in range(n) for e in range(2)]
            at = [pair * n + mm for mm in range(n)]
            keys = [kf[c, pl.ds(a, CB, stride=STEP), :].astype(BF16) for a in at]
            values = [vf[c, pl.ds(a, CB, stride=STEP), :] for a in at]
            swapped = [pltpu.roll(v, HEAD_DIM, 1) for v in values]
            both = {
                (mm, e): jnp.concatenate(
                    [
                        (
                            jnp.where(low_v, values[mm], swapped[mm])
                            if e == 0
                            else jnp.where(low_v, swapped[mm], values[mm])
                        ).astype(BF16),
                        ones,
                    ],
                    axis=1,
                )
                for mm, e in tags
            }
            scores = {
                (mm, e): nt_dot(qbt[e * 4 * LAT : (e + 1) * 4 * LAT, :], keys[mm]).reshape(4, LAT, CB)
                + bias[...][None]
                for mm, e in tags
            }
            peaks = {t: jnp.max(scores[t], axis=-1, keepdims=True) for t in tags}
            weights = {t: jnp.exp(scores[t] - peaks[t]).astype(BF16) for t in tags}
            for mm, e in tags:
                sums = jnp.dot(
                    weights[mm, e].reshape(4 * LAT, CB), both[mm, e], preferred_element_type=F32
                )
                for t in range(2):
                    a = sums[2 * t * LAT : (2 * t + 1) * LAT]
                    b = sums[(2 * t + 1) * LAT : (2 * t + 2) * LAT]
                    top = jnp.where(low, a[:, :CB], b[:, :CB])
                    bottom = jnp.where(low, a[:, CB:], b[:, CB:])
                    lanes = (e * 2 + t) * CB
                    att[pair * n + mm, :, lanes : lanes + CB] = (top / bottom).astype(BF16)
            return 0

        lax.fori_loop(0, STEP // n, some, 0)
        mixed = jnp.dot(
            att[...].reshape(STEP * LAT, D), w_out[...], preferred_element_type=F32
        ).reshape(STEP, LAT, D)
        latents = (q[...].astype(F32)[None] + mixed).reshape(STEP, CHAN, LG, D)
        for g in range(CHAN):
            lsend[g, c * STEP : (c + 1) * STEP] = latents[:, g].astype(BF16)
        for i, o in enumerate(OFFSETS):
            lat_copy(o, i, c).start()
        own_copy(c).start()

    for load in loads[8:]:
        load.wait()
    for c in range(CHUNKS):
        for i in reversed(range(len(OFFSETS))):
            o = OFFSETS[i]
            kv_copy(o, i, c).wait_recv()
            spread(kv_recv, from_peer(o), c)
        attend(c, 2)
        if c >= 2:
            forward(c - 2)
    for c in range(CHUNKS - 2, CHUNKS):
        forward(c)

    def regrid(source, l):
        for f in range(FT):
            turn[l, f, 0 : SCAN * LG] = source[:, :, f * CB : (f + 1) * CB].reshape(SCAN * LG, CB)
        for i in range(LG):
            for f in range(FT):
                grid_f[0, l, i, f, 8 : 8 + WIDE] = turn[l, f, pl.ds(i, WIDE, stride=LG), :]

    for c in range(CHUNKS):
        for s in range(CHAN):
            if not (s // 2 < DEEP or s // 2 >= LINES - DEEP):
                await_latents(s, c)
    for l in range(LINES):
        regrid(lrecv[l].reshape(SCAN, LG, D).astype(F32), l + DEEP)

    def halo_copy(c, half, way):
        return pltpu.make_async_remote_copy(
            src_ref=hsend.at[c - DEEP, half, way],
            dst_ref=hrecv.at[c - DEEP, half, way],
            send_sem=h_ssem.at[c - DEEP, half, way],
            recv_sem=h_rsem.at[c - DEEP, half, way],
            device_id=(ways[way], me),
            device_id_type=MESH,
        )

    def out_copy(l):
        return pltpu.make_async_copy(outb.at[l], out_h.at[l], out_sem.at[l])

    def clear_pair(c, half, out):
        now, later = c % 2, (c + 1) % 2
        apart = CLEAR - 1 - 2 * out
        own = out - DEEP + 1
        final = c == LAYERS - 1

        def stencil(n):
            l = out + n * apart
            for f in range(FT):
                for t in range(WIDE // 8):
                    cs = [coef[c, l, f, k, 8 * t : 8 * t + 8] for k in range(9)]
                    for i in range(HALF):
                        total = None
                        for k in range(9):
                            term = cs[k] * grid_f[
                                now, l + k // 3, half * HALF + i, f, pl.ds(7 + 8 * t + k % 3, 8), :
                            ]
                            total = term if total is None else total + term
                        st[n, i, 8 * t : 8 * t + 8, f * CB : (f + 1) * CB] = total.astype(BF16)

        def finish(n, update):
            l = out + n * apart
            for i in range(HALF):
                for f in range(FT):
                    lanes = slice(f * CB, (f + 1) * CB)
                    centre = grid_f[now, l + 1, half * HALF + i, f, 8 : 8 + WIDE]
                    cleared = (centre + update[i, :, lanes]).astype(BF16)
                    wide = cleared.astype(F32)
                    if final:
                        at = pl.ds(pl.multiple_of((half * HALF + i) * WIDE, WIDE), WIDE)
                        last[l - DEEP + 1, f, at] = wide
                    else:
                        if own < 0:
                            wide = jnp.where(comes[1 - n], wide, 0.0)
                        grid_f[later, l + 1, half * HALF + i, f, 8 : 8 + WIDE] = wide
                        if own == 0 and c + 1 >= DEEP:
                            hsend[c + 1 - DEEP, half, n, i, :, lanes] = cleared

        def mix(n):
            return jnp.dot(
                st[n].reshape(HALF * WIDE, D), w_mix[c], preferred_element_type=F32
            ).reshape(HALF, WIDE, D)

        stencil(0)
        first = mix(0)
        stencil(1)
        finish(0, first)
        finish(1, mix(1))
        if own == 0 and not final and c + 1 >= DEEP:
            for way in range(2):

                @pl.when(sends[way])
                def _():
                    halo_copy(c + 1, half, way).start()

    def finish_pair(first, apart):
        def columns(group, _):
            for d in range(COLUMNS):
                p = group * COLUMNS + d
                for n in range(2):
                    for f in range(FT):
                        rows = last[first + n * apart, f, pl.ds(p, LG, stride=WIDE), :]
                        outb[first + n * apart, p, :, f * CB : (f + 1) * CB] = rows.astype(BF16)
            return 0

        lax.fori_loop(0, SCAN // COLUMNS, columns, 0)
        for n in range(2):
            out_copy(first + n * apart).start()

    def take_near():
        for way in range(2):
            base = (DEEP + LINES, 0)[way]

            @pl.when(comes[way])
            def _():
                for n in range(CHUNKS):
                    near_copy(n, way).wait_recv()
                for d in range(DEEP):
                    regrid(near[way, d].reshape(SCAN, LG, D).astype(F32), base + d)

            @pl.when(jnp.logical_not(comes[way]))
            def _():
                for d in range(DEEP):
                    for i in range(LG):
                        grid_f[0, base + d, i, :, 8 : 8 + WIDE] = jnp.zeros((FT, WIDE, CB), F32)

    def take_halo(c, half, way):
        edge = (DEEP + LINES, DEEP - 1)[way]
        own = pl.ds(half * HALF, HALF)

        @pl.when(comes[way])
        def _():
            halo_copy(c, half, way).wait_recv()
            for f in range(FT):
                grid_f[c % 2, edge, own, f, 8 : 8 + WIDE] = hrecv[
                    c - DEEP, half, way, :, :, f * CB : (f + 1) * CB
                ].astype(F32)

        @pl.when(jnp.logical_not(comes[way]))
        def _():
            for f in range(FT):
                grid_f[c % 2, edge, own, f, 8 : 8 + WIDE] = jnp.zeros((HALF, WIDE, CB), F32)

    inner, outer = DEEP, DEEP - 1

    def clear_both(c, out):
        def one(half, _):
            clear_pair(c, half, out)
            return 0

        lax.fori_loop(0, 2, one, 0)

    def clear_with_halo(c):
        def one(half, _):
            for way in range(2):
                take_halo(c, half, way)
            clear_pair(c, half, outer)
            return 0

        lax.fori_loop(0, 2, one, 0)

    clear_both(0, inner)
    take_near()

    def up_to_halo(half, _):
        for c in range(DEEP):
            for out in range(outer, c - 1, -1):
                clear_pair(c, half, out)
        return 0

    lax.fori_loop(0, 2, up_to_halo, 0)
    clear_both(1, inner)
    clear_both(2, inner)
    finish_pair(1, 1)
    clear_with_halo(2)
    finish_pair(0, LINES - 1)

    for i, o in enumerate(OFFSETS):
        for c in range(CHUNKS):
            kv_copy(o, i, c).wait_send()
            lat_copy(o, i, c).wait_send()
    for way in range(2):

        @pl.when(sends[way])
        def _():
            vm_copy(way).wait_send()
            for c in range(CHUNKS):
                near_copy(c, way).wait_send()
            for c in range(DEEP, LAYERS):
                for half in range(2):
                    halo_copy(c, half, way).wait_send()

    for l in range(LINES):
        out_copy(l).wait()


def local(tracks, radiance, w_key, w_value, latent_query, band_blocks, band_count, valid_mask, w_out, conv_taps, w_mix):
    hbm = pl.BlockSpec(memory_space=pl.ANY)
    vmem = pltpu.VMEM
    dma = pltpu.SemaphoreType.DMA
    peers = len(OFFSETS)
    return pl.pallas_call(
        functools.partial(kernel, tracks),
        out_shape=jax.ShapeDtypeStruct((LINES, SCAN, LG, D), BF16),
        in_specs=[hbm] * 10,
        out_specs=hbm,
        scratch_shapes=[
            vmem((SCAN, BLK, LINES, CB), BF16),
            vmem((BLK, CB, CB), BF16),
            vmem((BLK, CB, CB), BF16),
            vmem((LAT, D), BF16),
            vmem((CHAN, MAXB), jnp.int32),
            pltpu.SMEM((CHAN,), jnp.int32),
            vmem((9, LINES, SCAN), jnp.int32),
            vmem((D, D), BF16),
            vmem((9, LAYERS, D), F32),
            vmem((LAYERS, D, D), BF16),
            vmem((2, 9, LINES, SCAN), jnp.int32),
            vmem((SCAN * BLK * LINES + 72, CB), F32),
            vmem((CHAN, CHUNKS, 2, BLK, STEP, CB), BF16),
            vmem((CHAN, CHUNKS, 2, BLK, STEP, CB), BF16),
            vmem((CHUNKS, CB * STEP, CB), F32),
            vmem((CHUNKS, CB * STEP, CB), F32),
            vmem((HEADS * LAT, CB), BF16),
            vmem((LAT, CB), F32),
            vmem((STEP, LAT, D), BF16),
            vmem((CHAN, ROWS, LG, D), BF16),
            vmem((LINES, 2, PER, LG, D), BF16),
            vmem((2, DEEP, 2, PER, LG, D), BF16),
            vmem((3, CB, CB), F32),
            vmem((CLEAR, 9, WIDE, CB), F32),
            vmem((LAYERS, CLEAR, FT, 9, WIDE, CB), F32),
            vmem((ALL, FT, WIDE * LG, CB), F32),
            vmem((2, ALL, LG, FT, WIDE + 16, CB), F32),
            vmem((2, HALF, WIDE, D), BF16),
            vmem((EXCH, 2, 2, HALF, WIDE, D), BF16),
            vmem((EXCH, 2, 2, HALF, WIDE, D), BF16),
            vmem((LINES, FT, LG * WIDE, CB), F32),
            vmem((LINES, SCAN, LG, D), BF16),
            dma((10,)),
            dma((CHUNKS, peers)), dma((CHUNKS, peers)),
            dma((CHUNKS, peers)), dma((CHUNKS, CHAN)),
            dma((CHUNKS, 2)), dma((CHUNKS, 2)),
            dma((2,)), dma((2,)),
            dma((EXCH, 2, 2)), dma((EXCH, 2, 2)),
            dma((LINES,)),
        ],
        compiler_params=pltpu.CompilerParams(
            collective_id=0, has_side_effects=True, vmem_limit_bytes=60 * 1024 * 1024
        ),
    )(
        jnp.transpose(radiance, (1, 2, 0, 3)), w_key, w_value, latent_query, band_blocks, band_count,
        jnp.transpose(valid_mask, (2, 0, 1)), w_out, jnp.transpose(conv_taps, (1, 0, 2)), w_mix,
    )


def solution(mesh):
    return jax.shard_map(
        functools.partial(local, mesh.shape["track"]),
        mesh=mesh,
        in_specs=(
            P("track", None, "chan", None),
            P("chan", None, None),
            P("chan", None, None),
            P(),
            P(),
            P(),
            P("track", None, None),
            P(),
            P(),
            P(),
        ),
        out_specs=P("track", None, "chan", None),
        check_vma=False,
    )
```
